512 devices in a mesh: bx: 16 (over x, z_hi), by: 4 (over z_lo, core), bz: 8 (over y).
Axes of the slice: x: 4, y: 8, z: 8 (z_hi: 4, z_lo: 2; z = z_hi * 2 + z_lo), core: 2. Of those that a mesh axis runs over, the one named last changes fastest.
Arguments:
- forcing: float32 [256, 256, 512], P('bx', 'bz', 'by'), may hold values from -6 to 6
- start: float32 [256, 256, 512], P('bx', 'bz', 'by'), may hold values from -2 to 2
- element_class_index: int32 [64, 64, 128], P('bx', 'bz', 'by'), may hold values from 0 to 15
- class_coef: float32 [3, 16], replicated, may hold values from 0.3 to 3
Outputs:
- solution: float32 [256, 256, 512], P('bx', 'bz', 'by')
- residual: float32 [256, 256, 512], P('bx', 'bz', 'by')
The draws below stay inside these ranges and needn't reach their ends.
All inputs are finite; a program needn't handle non-finite values.
Results may differ from the reference program's by a relative error of at most 0.015.
Values may be sent and summed in bfloat16 or wider, within the bound.
A program may use at most 64 MiB of HBM per device.

```python
import math
import jax
import jax.numpy as jnp
from jax import lax

COEF_CLASSES = 16
CYCLES = 2
ELEMENTS_X = 64
ELEMENTS_Z = 64
ELEMENTS_Y = 128
NX = 256
NZ = 256
NY = 512


def touch_ends(result, rng, smallest, largest):
    longest = result.shape.index(max(result.shape))
    spots = []
    for shift in (0, 1):
        where = [jax.random.randint(jax.random.fold_in(rng, axis), (), 0, length) for axis, length in enumerate(result.shape)]
        where[longest] = (where[longest] + shift) % result.shape[longest]
        spots.append(tuple(where))
    return result.at[spots[0]].set(smallest).at[spots[1]].set(largest)


def block_scale(key, shape, pieces, least, largest):
    level, own = 1.0, jax.random.fold_in(key, 6)
    for position, parts in pieces:
        draws = jnp.exp(jax.random.uniform(jax.random.fold_in(own, position), (parts,), jnp.float32, least / len(pieces), largest / len(pieces)))
        level = level * jnp.repeat(draws, shape[position] // parts).reshape([-1 if axis == position else 1 for axis in range(len(shape))])
    return level


def normal_values(stream_key, extent, width, most, shards=(), kind=jnp.bfloat16):
    entries = jax.random.normal(stream_key, extent, jnp.float32) * width
    if len(shards) > 0:
        entries = block_scale(stream_key, extent, shards, -0.22, 0.18) * entries
    return jnp.clip(entries, min=-most, max=most).astype(kind)


def setup_inputs(seed: int = 0) -> dict:
    key_of = jax.random.split(jax.random.key(seed), 5)
    return {
        "forcing": normal_values(key_of[0], (NX, NZ, NY), 1.0, 6.0, ((0, 16), (1, 8), (2, 4)), jnp.float32),
        "start": normal_values(key_of[1], (NX, NZ, NY), 0.3, 2.0, ((0, 16), (1, 8), (2, 4)), jnp.float32),
        "element_class_index": touch_ends(jax.random.randint(key_of[2], (ELEMENTS_X, ELEMENTS_Z, ELEMENTS_Y), 0, COEF_CLASSES), jax.random.fold_in(key_of[2], 1), 0, COEF_CLASSES - 1).astype(jnp.int32),
        "class_coef": jnp.clip(jnp.exp(jax.random.uniform(key_of[3], (3, COEF_CLASSES), jnp.float32, math.log(0.3), math.log(3.0))), 0.3, 3.0),
    }


FACE_PENALTY = 2.0
DAMPING = 0.6666666666666666

def face_factor(count):
    edges = jnp.arange(count + 1, dtype=jnp.int32)
    return jnp.where(edges % 4 == 0, FACE_PENALTY, 1.0).astype(jnp.float32)

def edge_weights(kappa_pad):
    inner_x = kappa_pad[:, 1:-1, 1:-1]
    weight_x = face_factor(inner_x.shape[0] - 2)[:, None, None] * ((inner_x[:-1] + inner_x[1:]) * 0.5)
    inner_z = kappa_pad[1:-1, :, 1:-1]
    weight_z = face_factor(inner_z.shape[1] - 2)[None, :, None] * ((inner_z[:, :-1] + inner_z[:, 1:]) * 0.5)
    inner_y = kappa_pad[1:-1, 1:-1, :]
    quadrature_weight_y = face_factor(inner_y.shape[2] - 2)[None, None, :] * ((inner_y[:, :, :-1] + inner_y[:, :, 1:]) * 0.5)
    return (weight_x, weight_z, quadrature_weight_y)

def operator_diagonal(weights, sigma_node):
    weight_x, weight_z, quadrature_weight_y = weights
    total = sigma_node + (weight_x[:-1] + weight_x[1:])
    total = total + (weight_z[:, :-1] + weight_z[:, 1:])
    return total + (quadrature_weight_y[:, :, :-1] + quadrature_weight_y[:, :, 1:])

def apply_operator(field_pad, weights, sigma_node):
    weight_x, weight_z, quadrature_weight_y = weights
    centre = field_pad[1:-1, 1:-1, 1:-1]
    total = sigma_node * centre
    total = total + weight_x[:-1] * (centre - field_pad[:-2, 1:-1, 1:-1]) + weight_x[1:] * (centre - field_pad[2:, 1:-1, 1:-1])
    total = total + weight_z[:, :-1] * (centre - field_pad[1:-1, :-2, 1:-1]) + weight_z[:, 1:] * (centre - field_pad[1:-1, 2:, 1:-1])
    total = total + quadrature_weight_y[:, :, :-1] * (centre - field_pad[1:-1, 1:-1, :-2]) + quadrature_weight_y[:, :, 1:] * (centre - field_pad[1:-1, 1:-1, 2:])
    return total

def node_field(element_values):
    return jnp.repeat(jnp.repeat(jnp.repeat(element_values, 4, 0), 4, 1), 4, 2)

def restrict_matrix():
    return jnp.array([[1.0, 2.0 / 3.0, 1.0 / 3.0, 0.0], [0.0, 1.0 / 3.0, 2.0 / 3.0, 1.0]], dtype=jnp.float32) * 0.5

def prolong_matrix():
    return jnp.array([[1.0, 0.0], [2.0 / 3.0, 1.0 / 3.0], [1.0 / 3.0, 2.0 / 3.0], [0.0, 1.0]], dtype=jnp.float32)

def restrict_field(field):
    count_x, count_z, count_y = (field.shape[0] // 4, field.shape[1] // 4, field.shape[2] // 4)
    blocks = field.reshape(count_x, 4, count_z, 4, count_y, 4)
    matrix = restrict_matrix()
    blocks = jnp.einsum('ai,pizjyk->pazjyk', matrix, blocks, precision=lax.Precision.HIGHEST)
    blocks = jnp.einsum('bj,pazjyk->pazbyk', matrix, blocks, precision=lax.Precision.HIGHEST)
    blocks = jnp.einsum('ck,pazbyk->pazbyc', matrix, blocks, precision=lax.Precision.HIGHEST)
    return blocks.reshape(2 * count_x, 2 * count_z, 2 * count_y)

def prolong_field(coarse):
    count_x, count_z, count_y = (coarse.shape[0] // 2, coarse.shape[1] // 2, coarse.shape[2] // 2)
    blocks = coarse.astype(jnp.float32).reshape(count_x, 2, count_z, 2, count_y, 2)
    matrix = prolong_matrix()
    blocks = jnp.einsum('ia,pazbyc->pizbyc', matrix, blocks, precision=lax.Precision.HIGHEST)
    blocks = jnp.einsum('jb,pizbyc->pizjyc', matrix, blocks, precision=lax.Precision.HIGHEST)
    blocks = jnp.einsum('kc,pizjyc->pizjyk', matrix, blocks, precision=lax.Precision.HIGHEST)
    return blocks.reshape(4 * count_x, 4 * count_z, 4 * count_y)

def sine_table(count):
    index_one = jnp.arange(count, dtype=jnp.int32) + 1
    product = (index_one[:, None] * index_one[None, :]).astype(jnp.float32)
    return (jnp.sin(product * (math.pi / (count + 1))) * math.sqrt(2.0 / (count + 1))).astype(jnp.bfloat16)

def spectrum_values(index_zero, count):
    return 2.0 - 2.0 * jnp.cos((index_zero + 1).astype(jnp.float32) * (math.pi / (count + 1)))

def transform(coarse, table, axis):
    moved = jnp.tensordot(table.astype(jnp.float32), coarse.astype(jnp.float32), axes=([1], [axis]), precision=lax.Precision.HIGHEST)
    return jnp.moveaxis(moved, 0, axis)

def reference(forcing, start, element_class_index, class_coef):
    kappa_node = node_field(class_coef[0][element_class_index])
    sigma_node = node_field(class_coef[1][element_class_index])
    beta_node = node_field(class_coef[2][element_class_index])
    weights = edge_weights(jnp.pad(kappa_node, 1))
    diagonal = operator_diagonal(weights, sigma_node)
    kappa_mean = jnp.mean(class_coef[0])
    sigma_mean = jnp.mean(class_coef[1])
    count_x, count_z, count_y = (2 * element_class_index.shape[0], 2 * element_class_index.shape[1], 2 * element_class_index.shape[2])
    table_x, table_z, table_y = (sine_table(count_x), sine_table(count_z), sine_table(count_y))
    eigen_x = spectrum_values(jnp.arange(count_x, dtype=jnp.int32), count_x)
    eigen_z = spectrum_values(jnp.arange(count_z, dtype=jnp.int32), count_z)
    eigen_y = spectrum_values(jnp.arange(count_y, dtype=jnp.int32), count_y)
    eigen_sum = kappa_mean * (eigen_x[:, None, None] + eigen_z[None, :, None] + eigen_y[None, None, :]) + sigma_mean

    def nonlinear_residual(solution):
        return forcing - apply_operator(jnp.pad(solution, 1), weights, sigma_node) - beta_node * solution * solution * solution
    solution = start
    for iteration in range(CYCLES):
        resid = nonlinear_residual(solution)
        smooth_one = DAMPING * resid / diagonal
        smooth_two = smooth_one + DAMPING * (resid - apply_operator(jnp.pad(smooth_one, 1), weights, sigma_node)) / diagonal
        coarse = restrict_field(resid).astype(jnp.bfloat16)
        coarse = transform(coarse, table_y, 2).astype(jnp.bfloat16)
        coarse = transform(coarse, table_z, 1).astype(jnp.bfloat16)
        coarse = (transform(coarse, table_x, 0) / eigen_sum).astype(jnp.bfloat16)
        coarse = transform(coarse, table_x, 0).astype(jnp.bfloat16)
        coarse = transform(coarse, table_z, 1).astype(jnp.bfloat16)
        coarse = transform(coarse, table_y, 2).astype(jnp.bfloat16)
        solution = solution + smooth_two + prolong_field(coarse)
    return (solution, nonlinear_residual(solution))
```

```python
import math

import jax
import jax.numpy as jnp
import numpy as np
from jax import lax
from jax.experimental import pallas as pl
from jax.experimental.pallas import tpu as pltpu
from jax.sharding import PartitionSpec as P

CYCLES = 2
DAMPING = 0.6666666666666666
NBX, NBY, NBZ = 16, 4, 8
CX, CZ, CY = 128, 128, 256
F32, BF16 = jnp.float32, jnp.bfloat16
MESH = pl.DeviceIdType.MESH
OFFSETS = sorted(
    ((a, b) for a in range(4) for b in range(4) if (a, b) != (0, 0)),
    key=lambda o: -(min(o[0], 4 - o[0]) + 2 * min(o[1], 4 - o[1])),
)


def rounded(value):
    return np.asarray(value, dtype=np.float64).astype(np.float32).astype(jnp.bfloat16)


def sine(count):
    index = np.arange(1, count + 1, dtype=np.float64)
    table = np.sin(np.outer(index, index) * (math.pi / (count + 1))) * math.sqrt(2.0 / (count + 1))
    return rounded(table).astype(np.float64)


def spectrum(count):
    return 2.0 - 2.0 * np.cos(np.arange(1, count + 1) * (math.pi / (count + 1)))


def tables():
    sine_x, sine_z, sine_y = sine(CX), sine(CZ), sine(CY)
    steps = np.array([[3.0, 2.0, 1.0, 0.0], [0.0, 1.0, 2.0, 3.0]])
    restrict_y = np.kron(np.eye(32), steps)
    restrict_y = np.concatenate([restrict_y, restrict_y], axis=1)
    restrict_z = np.kron(np.eye(64), steps).T
    prolong_z = np.concatenate([restrict_z, restrict_z], axis=1)
    blocks = sine_x.reshape(CX, NBX, 8)
    forward_x = np.zeros((2, CX, NBX, 2, 8))
    inverse_x = np.zeros((NBX, 2, 8, 2, CX))
    for member in range(2):
        forward_x[member, :, :, member, :] = blocks
        inverse_x[:, member, :, member, :] = sine_x.reshape(NBX, 8, CX)
    prolong_y = np.kron(np.eye(CY // 2), steps / 3.0)
    spread = (sine_y @ prolong_y).reshape(CY, NBY, 128).transpose(1, 0, 2)
    high = rounded(spread)
    low = rounded(spread - high.astype(np.float64))
    spread = np.stack([high, low], axis=1)
    plane = (spectrum(CX)[:, None] + spectrum(CZ)[None, :]).astype(np.float32)
    return (
        rounded(restrict_y),
        rounded(restrict_z),
        rounded(prolong_z),
        rounded(sine_y).reshape(NBY, 64, CY),
        rounded(sine_z),
        rounded(forward_x.reshape(256, 256)),
        rounded(inverse_x.reshape(NBX, 16, 256)),
        spread,
        plane,
        spectrum(CY).astype(np.float32),
    )


def turn(values, block):
    values = list(values)
    for bit in (4, 2, 1):
        low = (block & bit) == 0
        for first in range(8):
            if first & bit:
                continue
            second = first | bit
            one, two = values[first], values[second]
            values[first] = jnp.where(low, one, pltpu.roll(two, 16 * bit, 1))
            values[second] = jnp.where(low, pltpu.roll(one, 128 - 16 * bit, 1), two)
    return values


def kernel(
    forcing_hbm, start_hbm, class_ref, coef, eigen_y, ry_hbm, rz_hbm, pz_hbm, sy_hbm, sz_hbm,
    fx_hbm, ix_hbm, sp_hbm, plane_hbm,
    out_hbm, resid_hbm,
    f, s, z, r, inner, kap, beta, base, diag, dinv, wx, wxb, wzl, wzh, wzb, wyl, wyh, wyb,
    xh, zh, yh, zsend, ysend, kx, kz, ky, kzsend, kysend,
    ry, rz, pz, sy, sz, fx, ix, sp, plane, invlam, fine, swap,
    c0, va, vsend, xg, vb, vbsend, c5, last,
    load_sem, halo_s, halo_r, kap_s, kap_r, y1_s, y1_r, z1_s, z1_r, x_s, x_r, z2_s, z2_r, y2_s, y2_r,
):
    ib, iy, iz = lax.axis_index("bx"), lax.axis_index("by"), lax.axis_index("bz")
    loads = [
        pltpu.make_async_copy(src, dst, load_sem.at[i])
        for i, (src, dst) in enumerate(
            [
                (start_hbm, s.at[0]), (forcing_hbm, f), (ry_hbm, ry), (rz_hbm, rz), (pz_hbm, pz),
                (sy_hbm.at[iy], sy), (sz_hbm, sz), (fx_hbm, fx), (ix_hbm.at[ib], ix),
                (sp_hbm.at[iy], sp), (plane_hbm, plane),
            ]
        )
    ]
    for load in loads:
        load.start()

    def x_peer(offset):
        return lax.rem(ib // 4 + offset[0], 4) * 4 + lax.rem(lax.rem(ib, 4) + offset[1], 4)

    def z_peer(offset):
        return lax.rem(iz + offset, NBZ)

    def y_peer(offset):
        return lax.rem(iy + offset, NBY)

    z_order = (4, 3, 5, 2, 6, 1, 7)
    y_order = (2, 3, 1)
    barrier = pltpu.get_barrier_semaphore()
    for offset in OFFSETS:
        pl.semaphore_signal(barrier, inc=1, device_id={"bx": x_peer(offset)}, device_id_type=MESH)
    for offset in z_order:
        pl.semaphore_signal(barrier, inc=1, device_id={"bz": z_peer(offset)}, device_id_type=MESH)
    for offset in y_order:
        pl.semaphore_signal(barrier, inc=1, device_id={"by": y_peer(offset)}, device_id_type=MESH)

    row = lax.broadcasted_iota(jnp.int32, (32, 128), 0)
    lane = lax.broadcasted_iota(jnp.int32, (32, 128), 1)
    spread_y = (lax.broadcasted_iota(jnp.int32, (32, 128), 1) // 4 == row).astype(F32).astype(BF16)
    tall = lax.broadcasted_iota(jnp.int32, (128, 32), 0) // 4
    spread_z = (tall == lax.broadcasted_iota(jnp.int32, (128, 32), 1)).astype(F32).astype(BF16)
    labels = class_ref[...].astype(F32).astype(BF16)
    labels = jnp.dot(labels, spread_y, preferred_element_type=F32).astype(BF16)
    labels = jnp.dot(spread_z, labels, preferred_element_type=F32)
    kappa = jnp.zeros((128, 128), F32)
    sigma = jnp.zeros((128, 128), F32)
    cubic = jnp.zeros((128, 128), F32)
    for index in range(16):
        hit = labels == float(index)
        kappa = jnp.where(hit, coef[0, index], kappa)
        sigma = jnp.where(hit, coef[1, index], sigma)
        cubic = jnp.where(hit, coef[2, index], cubic)
    kap[...] = kappa.reshape(4, 32, 128)
    base[...] = sigma.reshape(4, 32, 128)
    beta[...] = cubic.reshape(4, 32, 128)
    kysend[...] = jnp.transpose(pltpu.roll(kappa, 1, 1))[0:8]
    kzsend[0:4] = kap[:, 0, :]
    kzsend[4:8] = kap[:, 31, :]

    def pack(field, slot):
        wide = lax.broadcasted_iota(jnp.int32, (128, 128), 1)
        edge = jnp.zeros((128, 128), F32)
        for e in range(4):
            part = field[4 * e : 4 * e + 4].reshape(128, 128)
            edge = jnp.where(wide // 2 == e, pltpu.roll(part, 1 + 2 * e, 1), edge)
        ysend[slot] = jnp.transpose(edge)[0:8]
        zsend[slot, 0] = field[:, 0, :]
        zsend[slot, 1] = field[:, 31, :]

    xa, xb = lax.rem(ib + 15, NBX), lax.rem(ib + 1, NBX)
    ya, yb = lax.rem(iy + 3, NBY), lax.rem(iy + 1, NBY)
    za, zb = lax.rem(iz + 7, NBZ), lax.rem(iz + 1, NBZ)

    def remote(src, dst, send, recv, device):
        return pltpu.make_async_remote_copy(
            src_ref=src, dst_ref=dst, send_sem=send, recv_sem=recv, device_id=device, device_id_type=MESH
        )

    def halo(field, slot, kind):
        ss, rs = halo_s.at[kind], halo_r.at[kind]
        return [
            remote(field.at[0], xh.at[slot, 1], ss.at[0], rs.at[0], {"bx": xa}),
            remote(field.at[15], xh.at[slot, 0], ss.at[1], rs.at[1], {"bx": xb}),
            remote(zsend.at[slot, 0], zh.at[slot, 1], ss.at[2], rs.at[2], {"bz": za}),
            remote(zsend.at[slot, 1], zh.at[slot, 0], ss.at[3], rs.at[3], {"bz": zb}),
            remote(ysend.at[slot], yh.at[slot, 1], ss.at[4], rs.at[4], {"by": ya}),
            remote(ysend.at[slot], yh.at[slot, 0], ss.at[5], rs.at[5], {"by": yb}),
        ]

    loads[0].wait()
    pack(s.at[0], 0)
    kappa_copies = [
        remote(kap.at[0], kx.at[1], kap_s.at[0], kap_r.at[0], {"bx": xa}),
        remote(kap.at[3], kx.at[0], kap_s.at[1], kap_r.at[1], {"bx": xb}),
        remote(kzsend, kz.at[1], kap_s.at[2], kap_r.at[2], {"bz": za}),
        remote(kzsend, kz.at[0], kap_s.at[3], kap_r.at[3], {"bz": zb}),
        remote(kysend, ky.at[1], kap_s.at[4], kap_r.at[4], {"by": ya}),
        remote(kysend, ky.at[0], kap_s.at[5], kap_r.at[5], {"by": yb}),
    ]
    pl.semaphore_wait(barrier, len(OFFSETS) + len(z_order) + len(y_order))
    for copy in kappa_copies:
        copy.start()
    copies = halo(s.at[0], 0, 0)
    for copy in copies:
        copy.start()

    zero = jnp.zeros((32, 128), F32)
    for e in range(4):
        k = kap[e]
        first, second, third = (row % 4 == 0), (row % 4 == 3), (lane % 4 == 0)
        zl = jnp.where(row == 0, zero, jnp.where(first, pltpu.roll(k, 1, 0) + k, k))
        zu = jnp.where(row == 31, zero, jnp.where(second, pltpu.roll(k, 31, 0) + k, k))
        yl = jnp.where(lane == 0, zero, jnp.where(third, pltpu.roll(k, 1, 1) + k, k))
        yu = jnp.where(lane == 127, zero, jnp.where(lane % 4 == 3, pltpu.roll(k, 127, 1) + k, k))
        wzl[e], wzh[e], wyl[e], wyh[e] = zl, zu, yl, yu
        base[e] = base[e] + ((zl + zu) + (yl + yu))
        for j in range(4):
            if j > 0:
                wx[4 * e + j] = k
            elif e > 0:
                wx[4 * e] = kap[e - 1] + k
    wx[0] = zero
    wx[16] = zero

    def inner_sum(field):
        def step(e, carry):
            zl, zu, yl, yu = wzl[e], wzh[e], wyl[e], wyh[e]
            for j in range(4):
                x = 4 * e + j
                v = field[x]
                total = zl * pltpu.roll(v, 1, 0) + zu * pltpu.roll(v, 31, 0)
                total = total + yl * pltpu.roll(v, 1, 1) + yu * pltpu.roll(v, 127, 1)
                total = total + wx[x] * field[lax.rem(x + 15, 16)]
                total = total + wx[x + 1] * field[lax.rem(x + 1, 16)]
                inner[x] = total
            return carry

        lax.fori_loop(0, 4, step, 0)

    inner_sum(s.at[0])

    kbar, sbar = coef[0, 0], coef[1, 0]
    for index in range(1, 16):
        kbar, sbar = kbar + coef[0, index], sbar + coef[1, index]
    kbar, sbar = kbar * 0.0625, sbar * 0.0625
    loads[10].wait()
    mode = iy * 64 + iz * 8
    for member in range(2):
        for pair in range(4):
            value = kbar * (plane[...] + eigen_y[mode + 2 * pair + member]) + sbar
            invlam[pl.ds(member * 128, 128), pl.ds(pair * 128, 128)] = 1.0 / value

    def inside(flag):
        return jnp.where(flag, 1.0, 0.0).astype(F32)

    x_in = (inside(ib > 0), inside(ib < NBX - 1))
    z_in = (inside(iz > 0), inside(iz < NBZ - 1))
    y_in = (inside(iy > 0), inside(iy < NBY - 1))
    for copy in kappa_copies:
        copy.wait()
    row8 = lax.broadcasted_iota(jnp.int32, (8, 128), 0)
    ends = []
    for side, e in ((0, 0), (1, 3)):
        weight = kap[e] + kx[side] * x_in[side]
        wxb[side] = weight * x_in[side]
        ends.append(weight)
    low_y = jnp.transpose(ky[0])[:, 0:1]
    high_y = jnp.transpose(ky[1])[:, 1:2]
    wide = lax.broadcasted_iota(jnp.int32, (128, 128), 1)
    outer = jnp.where(wide == 0, y_in[0], jnp.where(wide == 127, y_in[1], 0.0))
    other = jnp.where(wide == 0, jnp.broadcast_to(low_y, (128, 128)), jnp.broadcast_to(high_y, (128, 128)))
    edge_y = (wide == 0) | (wide == 127)
    edge_y = jnp.where(edge_y, kap[...].reshape(128, 128) + other * outer, 0.0)
    wyb[...] = (edge_y * outer).reshape(4, 32, 128)
    base[...] = base[...] + edge_y.reshape(4, 32, 128)
    for e in range(4):
        low = jnp.where(row8 == 0, kap[e, 0:8, :] + kz[0, 4 + e : 5 + e, :] * z_in[0], 0.0)
        high = jnp.where(row8 == 7, kap[e, 24:32, :] + kz[1, e : e + 1, :] * z_in[1], 0.0)
        wzb[0, e] = low * z_in[0]
        wzb[1, e] = high * z_in[1]
        base[e, 0:8, :] = base[e, 0:8, :] + low
        base[e, 24:32, :] = base[e, 24:32, :] + high
    for x in range(16):
        below = ends[0] if x == 0 else wx[x]
        above = ends[1] if x == 15 else wx[x + 1]
        total = base[x // 4] + (below + above)
        diag[x] = total
        dinv[x] = DAMPING / total

    def outer_sum(slot):
        inner[0] = inner[0] + wxb[0] * xh[slot, 0]
        inner[15] = inner[15] + wxb[1] * xh[slot, 1]
        low_y, high_y = jnp.transpose(yh[slot, 0]), jnp.transpose(yh[slot, 1])
        wide = lax.broadcasted_iota(jnp.int32, (128, 128), 1)
        for e in range(4):
            low = jnp.broadcast_to(low_y[:, 2 * e : 2 * e + 1], (128, 128))
            high = jnp.broadcast_to(high_y[:, 2 * e + 1 : 2 * e + 2], (128, 128))
            other = jnp.where(wide == 0, low, high).reshape(4, 32, 128)
            weight = wyb[e]
            for j in range(4):
                x = 4 * e + j
                inner[x] = inner[x] + weight * other[j]
                inner[x, 0:8, :] = inner[x, 0:8, :] + wzb[0, e] * zh[slot, 0, x : x + 1, :]
                inner[x, 24:32, :] = inner[x, 24:32, :] + wzb[1, e] * zh[slot, 1, x : x + 1, :]

    def residual(field, store):
        def step(e, carry):
            cube = beta[e]
            planes = []
            for j in range(4):
                x = 4 * e + j
                v = field[x]
                value = (f[x] - (diag[x] * v - inner[x])) - cube * v * v * v
                store[x] = value
                planes.append(value)
            return carry

        lax.fori_loop(0, 4, step, 0)

    block = lax.broadcasted_iota(jnp.int32, (8, 128), 1) // 16
    loads[1].wait()
    for load in loads[2:10]:
        load.wait()

    for cycle in range(CYCLES):
        for copy in copies:
            copy.wait()
        field = s.at[cycle]
        outer_sum(2 * cycle)
        residual(field, r)

        for e in range(4):
            one, two, three, four = (r[4 * e + j] for j in range(4))
            for half, value in ((0, 3.0 * one + 2.0 * two + three), (1, two + 2.0 * three + 3.0 * four)):
                high = value.astype(BF16)
                at = pl.ds((2 * e + half) * 32, 32)
                fine[at, 0:128] = high
                fine[at, 128:256] = (value - high.astype(F32)).astype(BF16)
        value = lax.dot_general(ry[...], fine[...], (((1,), (1,)), ((), ())), preferred_element_type=F32)
        high = value.astype(BF16)
        low = (value - high.astype(F32)).astype(BF16)
        value = jnp.dot(high, rz[...], preferred_element_type=F32) + jnp.dot(
            low, rz[...], preferred_element_type=F32
        )
        c0[cycle, iy] = (value * (1.0 / 216.0)).astype(BF16)
        sends = [
            remote(c0.at[cycle, iy], c0.at[cycle, iy], y1_s.at[cycle, y_peer(o)], y1_r.at[cycle, iy], {"by": y_peer(o)})
            for o in y_order
        ]
        for copy in sends:
            copy.start()

        smooth = z.at[cycle]
        smooth[...] = r[...] * dinv[...]
        pack(smooth, 2 * cycle + 1)
        smooth_copies = halo(smooth, 2 * cycle + 1, 1)

        for o in y_order:
            p = y_peer(o)
            remote(c0.at[cycle, p], c0.at[cycle, p], y1_s.at[cycle, p], y1_r.at[cycle, p], {"by": p}).wait_recv()
        value = jnp.dot(sy[...], c0[cycle].reshape(CY, 128), preferred_element_type=F32)
        vsend[cycle] = value.reshape(8, 8, 128).astype(BF16)
        z_sends = [
            remote(vsend.at[cycle, z_peer(o)], va.at[cycle, iz], z1_s.at[cycle, z_peer(o)], z1_r.at[cycle, iz], {"bz": z_peer(o)})
            for o in z_order
        ]
        for copy in z_sends:
            copy.start()
        va[cycle, iz] = vsend[cycle, iz]
        for copy in smooth_copies:
            copy.start()
        inner_sum(smooth)
        for copy in sends:
            copy.wait_send()
        for o in z_order:
            p = z_peer(o)
            remote(vsend.at[cycle, p], va.at[cycle, p], z1_s.at[cycle, p], z1_r.at[cycle, p], {"bz": p}).wait_recv()
        parts = turn([va[cycle, i].astype(F32) for i in range(8)], block)
        value = jnp.concatenate(parts, axis=0).astype(BF16)
        swap[...] = jnp.dot(value, sz[...], preferred_element_type=F32)
        value = jnp.concatenate([swap[pl.ds(m, 8, stride=8), :] for m in range(8)], axis=0)
        xg[cycle, ib] = value.reshape(4, 16, 128).astype(BF16)
        x_sends = [
            remote(xg.at[cycle, ib], xg.at[cycle, ib], x_s.at[cycle, x_peer(o)], x_r.at[cycle, ib], {"bx": x_peer(o)})
            for o in OFFSETS
        ]
        for copy in x_sends:
            copy.start()
        for copy in z_sends:
            copy.wait_send()

        for copy in smooth_copies:
            copy.wait()
        outer_sum(2 * cycle + 1)
        s[cycle + 1] = s[cycle] + ((2.0 - DAMPING) * smooth[...] + dinv[...] * inner[...])

        for o in OFFSETS:
            p = x_peer(o)
            remote(xg.at[cycle, p], xg.at[cycle, p], x_s.at[cycle, p], x_r.at[cycle, p], {"bx": p}).wait_recv()
        parts = []
        for half in range(2):
            value = jnp.concatenate(
                [xg[cycle, :, 2 * half + i, :, :].reshape(256, 128) for i in range(2)], axis=1
            )
            value = jnp.dot(fx[...], value, preferred_element_type=F32)
            value = (value * invlam[:, 256 * half : 256 * half + 256]).astype(BF16)
            value = jnp.dot(ix[...], value, preferred_element_type=F32)
            parts += [value[:, 0:128], value[:, 128:256]]
        value = jnp.concatenate(parts, axis=0).astype(BF16)
        swap[...] = jnp.dot(value, sz[...], preferred_element_type=F32)
        parts = turn([swap[pl.ds(i, 8, stride=8), :] for i in range(8)], block)
        for i in range(8):
            vbsend[cycle, i] = parts[i].astype(BF16)
        z_sends = [
            remote(vbsend.at[cycle, z_peer(o)], vb.at[cycle, iz], z2_s.at[cycle, z_peer(o)], z2_r.at[cycle, iz], {"bz": z_peer(o)})
            for o in z_order
        ]
        for copy in z_sends:
            copy.start()
        vb[cycle, iz] = vbsend[cycle, iz]
        for copy in x_sends:
            copy.wait_send()
        for o in z_order:
            p = z_peer(o)
            remote(vbsend.at[cycle, p], vb.at[cycle, p], z2_s.at[cycle, p], z2_r.at[cycle, p], {"bz": p}).wait_recv()
        c5[cycle, iy] = vb[cycle].astype(F32).reshape(64, 128).astype(BF16)
        sends = [
            remote(c5.at[cycle, iy], c5.at[cycle, iy], y2_s.at[cycle, y_peer(o)], y2_r.at[cycle, iy], {"by": y_peer(o)})
            for o in y_order
        ]
        for copy in sends:
            copy.start()
        for copy in z_sends:
            copy.wait_send()
        for o in y_order:
            p = y_peer(o)
            remote(c5.at[cycle, p], c5.at[cycle, p], y2_s.at[cycle, p], y2_r.at[cycle, p], {"by": p}).wait_recv()

        modes = c5[cycle].reshape(CY, 128)
        over = (((0,), (0,)), ((), ()))
        value = lax.dot_general(modes, sp[0], over, preferred_element_type=F32) + lax.dot_general(
            modes, sp[1], over, preferred_element_type=F32
        )
        high = value.astype(BF16)
        low = (value - high.astype(F32)).astype(BF16)
        value = jnp.dot(pz[...], jnp.concatenate([high, low], axis=0), preferred_element_type=F32)
        value = (value * (1.0 / 3.0)).reshape(8, 32, 128)
        after = s.at[cycle + 1]
        for e in range(4):
            one, two = value[2 * e], value[2 * e + 1]
            mixed = (one, one * (2.0 / 3.0) + two * (1.0 / 3.0), one * (1.0 / 3.0) + two * (2.0 / 3.0), two)
            for j in range(4):
                after[4 * e + j] = after[4 * e + j] + mixed[j]
        pack(after, 2 * cycle + 2)
        copies = halo(after, 2 * cycle + 2, 0)
        for copy in copies:
            copy.start()
        for copy in sends:
            copy.wait_send()
        inner_sum(after)

    store = pltpu.make_async_copy(s.at[CYCLES], out_hbm, load_sem.at[0])
    store.start()
    for copy in copies:
        copy.wait()
    outer_sum(2 * CYCLES)
    residual(s.at[CYCLES], last)
    final = pltpu.make_async_copy(last, resid_hbm, load_sem.at[1])
    final.start()
    store.wait()
    final.wait()


def body(forcing, start, element_class_index, class_coef):
    consts = [jnp.asarray(t) for t in tables()]
    eigen_y = consts.pop()
    full, brick = (16, 32, 128), (4, 32, 128)
    vmem = pltpu.VMEM
    dma = pltpu.SemaphoreType.DMA
    scratch = (
        [vmem(full, F32), vmem((3,) + full, F32), vmem((2,) + full, F32), vmem(full, F32), vmem(full, F32)]
        + [vmem(brick, F32)] * 3
        + [vmem(full, F32)] * 2
        + [vmem((17, 32, 128), F32), vmem((2, 32, 128), F32)]
        + [vmem(brick, F32)] * 2
        + [vmem((2, 4, 8, 128), F32)]
        + [vmem(brick, F32)] * 3
        + [vmem((5, 2, 32, 128), F32), vmem((5, 2, 16, 128), F32), vmem((5, 2, 8, 128), F32)]
        + [vmem((5, 2, 16, 128), F32), vmem((5, 8, 128), F32)]
        + [vmem((2, 32, 128), F32), vmem((2, 8, 128), F32), vmem((2, 8, 128), F32)]
        + [vmem((8, 128), F32), vmem((8, 128), F32)]
        + [vmem((64, 256), BF16), vmem((256, 128), BF16), vmem((256, 256), BF16), vmem((64, 256), BF16)]
        + [vmem((128, 128), BF16), vmem((256, 256), BF16), vmem((16, 256), BF16), vmem((2, 256, 128), BF16)]
        + [vmem((128, 128), F32), vmem((256, 512), F32), vmem((256, 256), BF16), vmem((64, 128), F32)]
        + [vmem((2, 4, 64, 128), BF16), vmem((2, 8, 8, 128), BF16), vmem((2, 8, 8, 128), BF16)]
        + [vmem((2, 16, 4, 16, 128), BF16), vmem((2, 8, 8, 128), BF16), vmem((2, 8, 8, 128), BF16)]
        + [vmem((2, 4, 64, 128), BF16), vmem(full, F32)]
        + [dma((11,)), dma((2, 6)), dma((2, 6)), dma((6,)), dma((6,))]
        + [dma((2, 4))] * 2
        + [dma((2, 8))] * 2
        + [dma((2, 16))] * 2
        + [dma((2, 8))] * 2
        + [dma((2, 4))] * 2
    )
    anywhere = pl.BlockSpec(memory_space=pl.ANY)
    scalar = pl.BlockSpec(memory_space=pltpu.SMEM)
    shape = jax.ShapeDtypeStruct(full, F32)
    return pl.pallas_call(
        kernel,
        out_shape=(shape, shape),
        in_specs=[anywhere, anywhere, pl.BlockSpec(memory_space=pltpu.VMEM), scalar, scalar] + [anywhere] * 9,
        out_specs=(anywhere, anywhere),
        scratch_shapes=scratch,
        compiler_params=pltpu.CompilerParams(collective_id=0, has_side_effects=True),
        name="cycles",
    )(forcing, start, element_class_index.reshape(32, 32), class_coef, eigen_y, *consts)


def solution(mesh):
    spec = P("bx", "bz", "by")
    return jax.shard_map(
        body, mesh=mesh, in_specs=(spec, spec, spec, P()), out_specs=(spec, spec), check_vma=False
    )
```

```python
import math

import jax
import jax.numpy as jnp
import numpy as np
from jax import lax
from jax.experimental import pallas as pl
from jax.experimental.pallas import tpu as pltpu
from jax.sharding import PartitionSpec as P

CYCLES = 2
DAMPING = 0.6666666666666666
NBX, NBY, NBZ = 16, 4, 8
CX, CZ, CY = 128, 128, 256
F32, BF16 = jnp.float32, jnp.bfloat16
MESH = pl.DeviceIdType.MESH
OFFSETS = sorted(
    ((a, b) for a in range(4) for b in range(4) if (a, b) != (0, 0)),
    key=lambda o: -(min(o[0], 4 - o[0]) + 2 * min(o[1], 4 - o[1])),
)


PLANE = [(a, b) for b in (4, 3, 5, 2, 6, 1, 7, 0) for a in (2, 3, 1, 0) if (a, b) != (0, 0)]


def rounded(value):
    return np.asarray(value, dtype=np.float64).astype(np.float32).astype(jnp.bfloat16)


def sine(count):
    index = np.arange(1, count + 1, dtype=np.float64)
    table = np.sin(np.outer(index, index) * (math.pi / (count + 1))) * math.sqrt(2.0 / (count + 1))
    return rounded(table).astype(np.float64)


def spectrum(count):
    return 2.0 - 2.0 * np.cos(np.arange(1, count + 1) * (math.pi / (count + 1)))


def split(value):
    high = rounded(value)
    return high, rounded(value - high.astype(np.float64))


def tables():
    sine_x, sine_z, sine_y = sine(CX), sine(CZ), sine(CY)
    steps = np.array([[3.0, 2.0, 1.0, 0.0], [0.0, 1.0, 2.0, 3.0]])
    restrict_z = np.kron(np.eye(64), steps)
    prolong_z = np.concatenate([restrict_z.T, restrict_z.T], axis=1)
    blocks = sine_x.reshape(CX, NBX, 8)
    forward_x = np.zeros((2, CX, NBX, 2, 8))
    inverse_x = np.zeros((NBX, 2, 16, 2, CX))
    for member in range(2):
        forward_x[member, :, :, member, :] = blocks
        inverse_x[:, member, :8, member, :] = sine_x.reshape(NBX, 8, CX)
        inverse_x[1:, member, 8, member, :] = sine_x[7:-1:8]
        inverse_x[:-1, member, 9, member, :] = sine_x[8::8]
    along_y = np.kron(np.eye(CY // 2), steps)
    spread = (sine_y @ along_y / 3.0).reshape(CY, NBY, 128).transpose(1, 0, 2)
    spread = np.concatenate(split(spread), axis=2)
    gather = (sine_y.reshape(CY, NBY, 64).transpose(1, 0, 2) @ np.kron(np.eye(32), steps)) / 6.0
    gather = np.concatenate(split(gather), axis=2)
    edge_y = np.zeros((NBY, 16, CY))
    edge_y[1:, 0] = sine_y[63:-1:64]
    edge_y[:-1, 1] = sine_y[64::64]
    halo = np.zeros((96, 128))
    for side in range(2):
        halo[32 * side : 32 * side + 32, 16 * side : 16 * side + 16] = np.kron(np.eye(8), steps).T
        halo[64 + 16 * side : 80 + 16 * side, 32 + 16 * side : 40 + 16 * side] = np.kron(np.eye(4), steps).T
    halo = np.concatenate([halo, halo], axis=1)
    plane_xz = np.kron(np.kron(np.eye(4), steps), np.kron(np.eye(8), steps))
    plane = (spectrum(CX)[:, None] + spectrum(CZ)[None, :]).astype(np.float32)
    return (
        rounded(restrict_z),
        rounded(prolong_z),
        gather,
        rounded(sine_z),
        rounded(forward_x.reshape(256, 256)),
        rounded(inverse_x.reshape(NBX, 32, 256)),
        spread,
        rounded(edge_y),
        rounded(halo),
        rounded(plane_xz),
        plane,
        spectrum(CY).astype(np.float32),
    )


def turn(values, block):
    values = list(values)
    for bit in (4, 2, 1):
        low = (block & bit) == 0
        for first in range(8):
            if first & bit:
                continue
            second = first | bit
            one, two = values[first], values[second]
            values[first] = jnp.where(low, one, pltpu.roll(two, 16 * bit, 1))
            values[second] = jnp.where(low, pltpu.roll(one, 128 - 16 * bit, 1), two)
    return values


def kernel(
    forcing_hbm, start_hbm, class_ref, coef, eigen_y, rz_hbm, pz_hbm, gy_hbm, sz_hbm,
    fx_hbm, ix_hbm, sp_hbm, ey_hbm, ph_hbm, kxz_hbm, plane_hbm,
    out_hbm, resid_hbm,
    f, s, z, r, inner, kap, beta, base, diag, dinv, wx, wxb, wzl, wzh, wzb, wyl, wyh, wyb,
    xh, zh, yh, zsend, ysend, kx, kz, ky, kzsend, kysend, yadd,
    rz, pz, gy, sz, fx, ix, sp, ey, ph, kxz, plane, invlam, fine, swap, wide_swap,
    va, vsend, xg, vb, vbsend, last,
    load_sem, halo_s, halo_r, kap_s, kap_r, z1_s, z1_r, x_s, x_r, z2_s, z2_r,
):
    ib, iy, iz = lax.axis_index("bx"), lax.axis_index("by"), lax.axis_index("bz")
    loads = [
        pltpu.make_async_copy(src, dst, load_sem.at[i])
        for i, (src, dst) in enumerate(
            [
                (start_hbm, s.at[0]), (forcing_hbm, f), (plane_hbm, plane), (rz_hbm, rz), (pz_hbm, pz),
                (gy_hbm.at[iy], gy), (sz_hbm, sz), (fx_hbm, fx), (ix_hbm.at[ib], ix),
                (sp_hbm.at[iy], sp), (ey_hbm.at[iy], ey), (ph_hbm, ph), (kxz_hbm, kxz),
            ]
        )
    ]
    for load in loads:
        load.start()

    def x_peer(offset):
        return lax.rem(ib // 4 + offset[0], 4) * 4 + lax.rem(lax.rem(ib, 4) + offset[1], 4)

    def plane_peer(offset):
        return lax.rem(iy + offset[0], NBY), lax.rem(iz + offset[1], NBZ)

    barrier = pltpu.get_barrier_semaphore()
    for offset in OFFSETS:
        pl.semaphore_signal(barrier, inc=1, device_id={"bx": x_peer(offset)}, device_id_type=MESH)
    for offset in PLANE:
        py, pz_ = plane_peer(offset)
        pl.semaphore_signal(barrier, inc=1, device_id={"by": py, "bz": pz_}, device_id_type=MESH)

    row = lax.broadcasted_iota(jnp.int32, (32, 128), 0)
    lane = lax.broadcasted_iota(jnp.int32, (32, 128), 1)
    spread_y = (lax.broadcasted_iota(jnp.int32, (32, 128), 1) // 4 == row).astype(F32).astype(BF16)
    tall = lax.broadcasted_iota(jnp.int32, (128, 32), 0) // 4
    spread_z = (tall == lax.broadcasted_iota(jnp.int32, (128, 32), 1)).astype(F32).astype(BF16)
    labels = class_ref[...].astype(F32).astype(BF16)
    labels = jnp.dot(labels, spread_y, preferred_element_type=F32).astype(BF16)
    labels = jnp.dot(spread_z, labels, preferred_element_type=F32)
    kappa = jnp.zeros((128, 128), F32)
    sigma = jnp.zeros((128, 128), F32)
    cubic = jnp.zeros((128, 128), F32)
    for index in range(16):
        hit = labels == float(index)
        kappa = jnp.where(hit, coef[0, index], kappa)
        sigma = jnp.where(hit, coef[1, index], sigma)
        cubic = jnp.where(hit, coef[2, index], cubic)
    kap[...] = kappa.reshape(4, 32, 128)
    base[...] = sigma.reshape(4, 32, 128)
    beta[...] = cubic.reshape(4, 32, 128)
    kysend[...] = jnp.transpose(pltpu.roll(kappa, 1, 1))[0:8]
    kzsend[0:4] = kap[:, 0, :]
    kzsend[4:8] = kap[:, 31, :]

    def pack(field, slot):
        wide = lax.broadcasted_iota(jnp.int32, (128, 128), 1)
        edge = jnp.zeros((128, 128), F32)
        for e in range(4):
            part = field[4 * e : 4 * e + 4].reshape(128, 128)
            edge = jnp.where(wide // 2 == e, pltpu.roll(part, 1 + 2 * e, 1), edge)
        ysend[slot] = jnp.transpose(edge)[0:8]
        zsend[slot, 0] = field[:, 0, :]
        zsend[slot, 1] = field[:, 31, :]

    xa, xb = lax.rem(ib + 15, NBX), lax.rem(ib + 1, NBX)
    ya, yb = lax.rem(iy + 3, NBY), lax.rem(iy + 1, NBY)
    za, zb = lax.rem(iz + 7, NBZ), lax.rem(iz + 1, NBZ)

    def remote(src, dst, send, recv, device):
        return pltpu.make_async_remote_copy(
            src_ref=src, dst_ref=dst, send_sem=send, recv_sem=recv, device_id=device, device_id_type=MESH
        )

    def halo(field, slot, kind):
        ss, rs = halo_s.at[kind], halo_r.at[kind]
        return [
            remote(field.at[0], xh.at[slot, 1], ss.at[0], rs.at[0], {"bx": xa}),
            remote(field.at[15], xh.at[slot, 0], ss.at[1], rs.at[1], {"bx": xb}),
            remote(zsend.at[slot, 0], zh.at[slot, 1], ss.at[2], rs.at[2], {"bz": za}),
            remote(zsend.at[slot, 1], zh.at[slot, 0], ss.at[3], rs.at[3], {"bz": zb}),
            remote(ysend.at[slot], yh.at[slot, 1], ss.at[4], rs.at[4], {"by": ya}),
            remote(ysend.at[slot], yh.at[slot, 0], ss.at[5], rs.at[5], {"by": yb}),
        ]

    loads[0].wait()
    pack(s.at[0], 0)
    kappa_copies = [
        remote(kap.at[0], kx.at[1], kap_s.at[0], kap_r.at[0], {"bx": xa}),
        remote(kap.at[3], kx.at[0], kap_s.at[1], kap_r.at[1], {"bx": xb}),
        remote(kzsend, kz.at[1], kap_s.at[2], kap_r.at[2], {"bz": za}),
        remote(kzsend, kz.at[0], kap_s.at[3], kap_r.at[3], {"bz": zb}),
        remote(kysend, ky.at[1], kap_s.at[4], kap_r.at[4], {"by": ya}),
        remote(kysend, ky.at[0], kap_s.at[5], kap_r.at[5], {"by": yb}),
    ]
    pl.semaphore_wait(barrier, len(OFFSETS) + len(PLANE))
    for copy in kappa_copies:
        copy.start()
    copies = halo(s.at[0], 0, 0)
    for copy in copies:
        copy.start()

    zero = jnp.zeros((32, 128), F32)
    for e in range(4):
        k = kap[e]
        first, second, third = (row % 4 == 0), (row % 4 == 3), (lane % 4 == 0)
        zl = jnp.where(row == 0, zero, jnp.where(first, pltpu.roll(k, 1, 0) + k, k))
        zu = jnp.where(row == 31, zero, jnp.where(second, pltpu.roll(k, 31, 0) + k, k))
        yl = jnp.where(lane == 0, zero, jnp.where(third, pltpu.roll(k, 1, 1) + k, k))
        yu = jnp.where(lane == 127, zero, jnp.where(lane % 4 == 3, pltpu.roll(k, 127, 1) + k, k))
        wzl[e], wzh[e], wyl[e], wyh[e] = zl, zu, yl, yu
        base[e] = base[e] + ((zl + zu) + (yl + yu))
        for j in range(4):
            if j > 0:
                wx[4 * e + j] = k
            elif e > 0:
                wx[4 * e] = kap[e - 1] + k
    wx[0] = zero
    wx[16] = zero

    def inner_sum(field):
        def step(e, carry):
            zl, zu, yl, yu = wzl[e], wzh[e], wyl[e], wyh[e]
            for j in range(4):
                x = 4 * e + j
                v = field[x]
                total = zl * pltpu.roll(v, 1, 0) + zu * pltpu.roll(v, 31, 0)
                total = total + yl * pltpu.roll(v, 1, 1) + yu * pltpu.roll(v, 127, 1)
                total = total + wx[x] * field[lax.rem(x + 15, 16)]
                total = total + wx[x + 1] * field[lax.rem(x + 1, 16)]
                inner[x] = total
            return carry

        lax.fori_loop(0, 4, step, 0)

    inner_sum(s.at[0])

    kbar, sbar = coef[0, 0], coef[1, 0]
    for index in range(1, 16):
        kbar, sbar = kbar + coef[0, index], sbar + coef[1, index]
    kbar, sbar = kbar * 0.0625, sbar * 0.0625
    loads[2].wait()
    mode = iy * 64 + iz * 8
    for member in range(2):
        for pair in range(4):
            value = kbar * (plane[...] + eigen_y[mode + 2 * pair + member]) + sbar
            invlam[pl.ds(member * 128, 128), pl.ds(pair * 128, 128)] = 1.0 / value

    def inside(flag):
        return jnp.where(flag, 1.0, 0.0).astype(F32)

    x_in = (inside(ib > 0), inside(ib < NBX - 1))
    z_in = (inside(iz > 0), inside(iz < NBZ - 1))
    y_in = (inside(iy > 0), inside(iy < NBY - 1))
    for copy in kappa_copies:
        copy.wait()
    row8 = lax.broadcasted_iota(jnp.int32, (8, 128), 0)
    ends = []
    for side, e in ((0, 0), (1, 3)):
        weight = kap[e] + kx[side] * x_in[side]
        wxb[side] = weight * x_in[side]
        ends.append(weight)
    low_y = jnp.transpose(ky[0])[:, 0:1]
    high_y = jnp.transpose(ky[1])[:, 1:2]
    wide = lax.broadcasted_iota(jnp.int32, (128, 128), 1)
    outer = jnp.where(wide == 0, y_in[0], jnp.where(wide == 127, y_in[1], 0.0))
    other = jnp.where(wide == 0, jnp.broadcast_to(low_y, (128, 128)), jnp.broadcast_to(high_y, (128, 128)))
    edge_y = (wide == 0) | (wide == 127)
    edge_y = jnp.where(edge_y, kap[...].reshape(128, 128) + other * outer, 0.0)
    wyb[...] = (edge_y * outer).reshape(4, 32, 128)
    base[...] = base[...] + edge_y.reshape(4, 32, 128)
    for e in range(4):
        low = jnp.where(row8 == 0, kap[e, 0:8, :] + kz[0, 4 + e : 5 + e, :] * z_in[0], 0.0)
        high = jnp.where(row8 == 7, kap[e, 24:32, :] + kz[1, e : e + 1, :] * z_in[1], 0.0)
        wzb[0, e] = low * z_in[0]
        wzb[1, e] = high * z_in[1]
        base[e, 0:8, :] = base[e, 0:8, :] + low
        base[e, 24:32, :] = base[e, 24:32, :] + high
    for x in range(16):
        below = ends[0] if x == 0 else wx[x]
        above = ends[1] if x == 15 else wx[x + 1]
        total = base[x // 4] + (below + above)
        diag[x] = total
        dinv[x] = DAMPING / total

    def outer_sum(x_sides, z_sides, y_rows):
        inner[0] = inner[0] + wxb[0] * x_sides[0]
        inner[15] = inner[15] + wxb[1] * x_sides[1]
        columns = jnp.transpose(y_rows)
        wide = lax.broadcasted_iota(jnp.int32, (128, 128), 1)
        for e in range(4):
            low = jnp.broadcast_to(columns[:, e : e + 1], (128, 128))
            high = jnp.broadcast_to(columns[:, 4 + e : 5 + e], (128, 128))
            other = jnp.where(wide == 0, low, high).reshape(4, 32, 128)
            weight = wyb[e]
            for j in range(4):
                x = 4 * e + j
                inner[x] = inner[x] + weight * other[j]
                inner[x, 0:8, :] = inner[x, 0:8, :] + wzb[0, e] * z_sides[0][x : x + 1, :]
                inner[x, 24:32, :] = inner[x, 24:32, :] + wzb[1, e] * z_sides[1][x : x + 1, :]

    def arrived(slot):
        for e in range(4):
            yadd[e : e + 1, :] = yh[slot, 0, 2 * e : 2 * e + 1, :]
            yadd[4 + e : 5 + e, :] = yh[slot, 1, 2 * e + 1 : 2 * e + 2, :]
        return [xh[slot, 0], xh[slot, 1]], [zh[slot, 0], zh[slot, 1]], yadd[...]

    def residual(field, store):
        def step(e, carry):
            cube = beta[e]
            planes = []
            for j in range(4):
                x = 4 * e + j
                v = field[x]
                value = (f[x] - (diag[x] * v - inner[x])) - cube * v * v * v
                store[x] = value
                planes.append(value)
            return carry

        lax.fori_loop(0, 4, step, 0)

    block = lax.broadcasted_iota(jnp.int32, (8, 128), 1) // 16
    loads[1].wait()
    for load in loads[3:]:
        load.wait()
    for copy in copies:
        copy.wait()
    outer_sum(*arrived(0))
    residual(s.at[0], r)
    lane8 = lax.broadcasted_iota(jnp.int32, (8, 128), 1)
    me = iy * NBZ + iz

    for cycle in range(CYCLES):
        for e in range(4):
            one, two, three, four = (r[4 * e + j] for j in range(4))
            for half, value in ((0, 3.0 * one + 2.0 * two + three), (1, two + 2.0 * three + 3.0 * four)):
                high = value.astype(BF16)
                at = pl.ds((2 * e + half) * 32, 32)
                fine[at, 0:128] = high
                fine[at, 128:256] = (value - high.astype(F32)).astype(BF16)
        value = jnp.dot(rz[...], fine[...], preferred_element_type=F32)
        value = ((value[:, 0:128] + value[:, 128:256]) * (1.0 / 36.0)).astype(BF16)
        value = jnp.concatenate([value, value], axis=1)
        value = lax.dot_general(gy[...], value, (((1,), (1,)), ((), ())), preferred_element_type=F32)
        vsend[cycle] = value.reshape(32, 8, 128).astype(BF16)

        def forward(offset, receive=False):
            py, pz_ = plane_peer(offset)
            p = py * NBZ + pz_
            here = p if receive else me
            return remote(
                vsend.at[cycle, p], va.at[cycle, here], z1_s.at[cycle, p], z1_r.at[cycle, here], {"by": py, "bz": pz_}
            )

        plane_sends = [forward(o) for o in PLANE]
        for copy in plane_sends:
            copy.start()
        va[cycle, me] = vsend[cycle, me]

        smooth = z.at[cycle]
        smooth[...] = r[...] * dinv[...]
        pack(smooth, 2 * cycle + 1)
        smooth_copies = halo(smooth, 2 * cycle + 1, 1)
        for copy in smooth_copies:
            copy.start()
        inner_sum(smooth)
        for o in PLANE:
            forward(o, True).wait_recv()
        parts = []
        for i in range(8):
            one, two, three, four = (va[cycle, 8 * j + i].astype(F32) for j in range(4))
            parts.append((one + two) + (three + four))
        value = jnp.concatenate(turn(parts, block), axis=0).astype(BF16)
        swap[...] = jnp.dot(value, sz[...], preferred_element_type=F32)
        value = jnp.concatenate([swap[pl.ds(m, 8, stride=8), :] for m in range(8)], axis=0)
        xg[cycle, ib] = value.reshape(4, 16, 128).astype(BF16)
        x_sends = [
            remote(xg.at[cycle, ib], xg.at[cycle, ib], x_s.at[cycle, x_peer(o)], x_r.at[cycle, ib], {"bx": x_peer(o)})
            for o in OFFSETS
        ]
        for copy in x_sends:
            copy.start()
        for copy in plane_sends:
            copy.wait_send()

        after = s.at[cycle + 1]
        for copy in smooth_copies:
            copy.wait()
        outer_sum(*arrived(2 * cycle + 1))
        after[...] = s[cycle] + ((2.0 - DAMPING) * smooth[...] + dinv[...] * inner[...])
        pack(after, 2 * cycle + 2)
        copies = halo(after, 2 * cycle + 2, 0)
        for copy in copies:
            copy.start()

        for o in OFFSETS:
            p = x_peer(o)
            remote(xg.at[cycle, p], xg.at[cycle, p], x_s.at[cycle, p], x_r.at[cycle, p], {"bx": p}).wait_recv()
        parts = []
        for half in range(2):
            value = jnp.concatenate(
                [xg[cycle, :, 2 * half + i, :, :].reshape(256, 128) for i in range(2)], axis=1
            )
            value = jnp.dot(fx[...], value, preferred_element_type=F32)
            value = (value * invlam[:, 256 * half : 256 * half + 256]).astype(BF16)
            value = jnp.dot(ix[...], value, preferred_element_type=F32)
            parts += [value[:, 0:128], value[:, 128:256]]
        value = jnp.concatenate(parts, axis=0).astype(BF16)
        wide_swap[...] = jnp.dot(value, sz[...], preferred_element_type=F32)
        lines = [wide_swap[pl.ds(i, 8, stride=16), :] for i in range(10)]
        low = high = none = jnp.zeros((8, 128), F32)
        for i in range(8):
            low = jnp.where(lane8 % 16 == i, pltpu.roll(lines[i], 1 + i, 1), low)
            high = jnp.where(lane8 % 16 == i, pltpu.roll(lines[i], 112 + i, 1), high)
        own = turn(lines[0:8], block)
        beyond = turn([lines[8], lines[9], low, high, none, none, none, none], block)
        for i in range(8):
            vbsend[cycle, i, 0] = own[i].astype(BF16)
            vbsend[cycle, i, 1] = beyond[i].astype(BF16)

        def backward(offset, receive=False):
            py, pz_ = plane_peer(offset)
            p = py * NBZ + pz_
            here = p if receive else me
            return remote(
                vbsend.at[cycle, pz_], vb.at[cycle, here], z2_s.at[cycle, p], z2_r.at[cycle, here], {"by": py, "bz": pz_}
            )

        plane_sends = [backward(o) for o in PLANE]
        for copy in plane_sends:
            copy.start()
        vb[cycle, me] = vbsend[cycle, iz]
        for copy in x_sends:
            copy.wait_send()
        for copy in copies:
            copy.wait()
        x_sides, z_sides, y_rows = arrived(2 * cycle + 2)
        for o in PLANE:
            backward(o, True).wait_recv()

        own = vb[cycle, :, 0].astype(F32).reshape(CY, 128).astype(BF16)
        beyond = vb[cycle, :, 1].astype(F32).reshape(CY, 128).astype(BF16)
        value = lax.dot_general(
            jnp.concatenate([own, beyond], axis=1), sp[...], (((0,), (0,)), ((), ())), preferred_element_type=F32
        )
        value = value[:, 0:128] + value[:, 128:256]
        high = value.astype(BF16)
        low = (value - high.astype(F32)).astype(BF16)
        value = jnp.dot(pz[...], jnp.concatenate([high[0:128], low[0:128]], axis=0), preferred_element_type=F32)
        value = (value * (1.0 / 3.0)).reshape(8, 32, 128)
        outside = jnp.dot(ph[...], jnp.concatenate([high[128:256], low[128:256]], axis=0), preferred_element_type=F32)
        outside = outside * (1.0 / 3.0)
        edge = jnp.dot(ey[...], own, preferred_element_type=F32)
        high = edge.astype(BF16)
        low = (edge - high.astype(F32)).astype(BF16)
        edge = jnp.dot(jnp.concatenate([high, low], axis=0), kxz[...], preferred_element_type=F32)
        edge = (edge[0:8] + edge[16:24]) * (1.0 / 9.0)
        for e in range(4):
            one, two = value[2 * e], value[2 * e + 1]
            mixed = (one, one * (2.0 / 3.0) + two * (1.0 / 3.0), one * (1.0 / 3.0) + two * (2.0 / 3.0), two)
            for j in range(4):
                after[4 * e + j] = after[4 * e + j] + mixed[j]
            yadd[e : e + 1, :] = edge[0:1, 128 * e : 128 * e + 128]
            yadd[4 + e : 5 + e, :] = edge[1:2, 128 * e : 128 * e + 128]
        if cycle == CYCLES - 1:
            store = pltpu.make_async_copy(s.at[CYCLES], out_hbm, load_sem.at[0])
            store.start()
        for copy in plane_sends:
            copy.wait_send()
        inner_sum(after)
        outer_sum(
            [x_sides[0] + outside[0:32], x_sides[1] + outside[32:64]],
            [z_sides[0] + outside[64:80], z_sides[1] + outside[80:96]],
            y_rows + yadd[...],
        )
        residual(after, last if cycle == CYCLES - 1 else r)

    final = pltpu.make_async_copy(last, resid_hbm, load_sem.at[1])
    final.start()
    store.wait()
    final.wait()


def body(forcing, start, element_class_index, class_coef):
    consts = [jnp.asarray(t) for t in tables()]
    eigen_y = consts.pop()
    full, brick = (16, 32, 128), (4, 32, 128)
    vmem = pltpu.VMEM
    dma = pltpu.SemaphoreType.DMA
    scratch = (
        [vmem(full, F32), vmem((3,) + full, F32), vmem((2,) + full, F32), vmem(full, F32), vmem(full, F32)]
        + [vmem(brick, F32)] * 3
        + [vmem(full, F32)] * 2
        + [vmem((17, 32, 128), F32), vmem((2, 32, 128), F32)]
        + [vmem(brick, F32)] * 2
        + [vmem((2, 4, 8, 128), F32)]
        + [vmem(brick, F32)] * 3
        + [vmem((5, 2, 32, 128), F32), vmem((5, 2, 16, 128), F32), vmem((5, 2, 8, 128), F32)]
        + [vmem((5, 2, 16, 128), F32), vmem((5, 8, 128), F32)]
        + [vmem((2, 32, 128), F32), vmem((2, 8, 128), F32), vmem((2, 8, 128), F32)]
        + [vmem((8, 128), F32)] * 3
        + [vmem((128, 256), BF16), vmem((256, 256), BF16), vmem((256, 256), BF16), vmem((128, 128), BF16)]
        + [vmem((256, 256), BF16), vmem((32, 256), BF16), vmem((256, 256), BF16), vmem((16, 256), BF16)]
        + [vmem((96, 256), BF16), vmem((128, 512), BF16), vmem((128, 128), F32), vmem((256, 512), F32)]
        + [vmem((256, 256), BF16), vmem((64, 128), F32), vmem((128, 128), F32)]
        + [vmem((2, 32, 8, 128), BF16), vmem((2, 32, 8, 128), BF16), vmem((2, 16, 4, 16, 128), BF16)]
        + [vmem((2, 32, 2, 8, 128), BF16), vmem((2, 8, 2, 8, 128), BF16), vmem(full, F32)]
        + [dma((13,)), dma((2, 6)), dma((2, 6)), dma((6,)), dma((6,))]
        + [dma((2, 32))] * 2
        + [dma((2, 16))] * 2
        + [dma((2, 32))] * 2
    )
    anywhere = pl.BlockSpec(memory_space=pl.ANY)
    scalar = pl.BlockSpec(memory_space=pltpu.SMEM)
    shape = jax.ShapeDtypeStruct(full, F32)
    return pl.pallas_call(
        kernel,
        out_shape=(shape, shape),
        in_specs=[anywhere, anywhere, pl.BlockSpec(memory_space=pltpu.VMEM), scalar, scalar] + [anywhere] * 11,
        out_specs=(anywhere, anywhere),
        scratch_shapes=scratch,
        compiler_params=pltpu.CompilerParams(collective_id=0, has_side_effects=True),
        name="cycles",
    )(forcing, start, element_class_index.reshape(32, 32), class_coef, eigen_y, *consts)


def solution(mesh):
    spec = P("bx", "bz", "by")
    return jax.shard_map(
        body, mesh=mesh, in_specs=(spec, spec, spec, P()), out_specs=(spec, spec), check_vma=False
    )
```

```python
import math

import jax
import jax.numpy as jnp
import numpy as np
from jax import lax
from jax.experimental import pallas as pl
from jax.experimental.pallas import tpu as pltpu
from jax.sharding import PartitionSpec as P

CYCLES = 2
DAMPING = 0.6666666666666666
NBX, NBY, NBZ = 16, 4, 8
CX, CZ, CY = 128, 128, 256
F32, BF16 = jnp.float32, jnp.bfloat16
MESH = pl.DeviceIdType.MESH
OFFSETS = sorted(
    ((a, b) for a in range(4) for b in range(4) if (a, b) != (0, 0)),
    key=lambda o: -(min(o[0], 4 - o[0]) + 2 * min(o[1], 4 - o[1])),
)


PLANE = [(a, b) for b in (4, 3, 5, 2, 6, 1, 7, 0) for a in (2, 3, 1, 0) if (a, b) != (0, 0)]


ROWS = {
    "rz": slice(0, 128), "pz": slice(128, 384), "fx": slice(384, 640),
    "ph": slice(640, 736), "kxz": slice(736, 992), "sz": slice(992, 1120),
}


def rounded(value):
    return np.asarray(value, dtype=np.float64).astype(np.float32).astype(jnp.bfloat16)


def sine(count):
    index = np.arange(1, count + 1, dtype=np.float64)
    table = np.sin(np.outer(index, index) * (math.pi / (count + 1))) * math.sqrt(2.0 / (count + 1))
    return rounded(table).astype(np.float64)


def spectrum(count):
    return 2.0 - 2.0 * np.cos(np.arange(1, count + 1) * (math.pi / (count + 1)))


def split(value):
    high = rounded(value)
    return high, rounded(value - high.astype(np.float64))


def tables():
    sine_x, sine_z, sine_y = sine(CX), sine(CZ), sine(CY)
    steps = np.array([[3.0, 2.0, 1.0, 0.0], [0.0, 1.0, 2.0, 3.0]])
    restrict_z = np.kron(np.eye(64), steps)
    prolong_z = np.concatenate([restrict_z.T, restrict_z.T], axis=1)
    blocks = sine_x.reshape(CX, NBX, 8)
    forward_x = np.zeros((2, CX, NBX, 2, 8))
    inverse_x = np.zeros((NBX, 2, 16, 2, CX))
    for member in range(2):
        forward_x[member, :, :, member, :] = blocks
        inverse_x[:, member, :8, member, :] = sine_x.reshape(NBX, 8, CX)
        inverse_x[1:, member, 8, member, :] = sine_x[7:-1:8]
        inverse_x[:-1, member, 9, member, :] = sine_x[8::8]
    along_y = np.kron(np.eye(CY // 2), steps)
    spread = (sine_y @ along_y / 3.0).reshape(CY, NBY, 128).transpose(1, 0, 2)
    spread = np.concatenate(split(spread), axis=2)
    gather = (sine_y.reshape(CY, NBY, 64).transpose(1, 0, 2) @ np.kron(np.eye(32), steps)) / 6.0
    gather = np.concatenate(split(gather), axis=2)
    edge_y = np.zeros((NBY, 16, CY))
    edge_y[1:, 0] = sine_y[63:-1:64]
    edge_y[:-1, 1] = sine_y[64::64]
    halo = np.zeros((96, 128))
    for side in range(2):
        halo[32 * side : 32 * side + 32, 16 * side : 16 * side + 16] = np.kron(np.eye(8), steps).T
        halo[64 + 16 * side : 80 + 16 * side, 32 + 16 * side : 40 + 16 * side] = np.kron(np.eye(4), steps).T
    halo = np.concatenate([halo, halo], axis=1)
    plane_xz = np.kron(np.kron(np.eye(4), steps), np.kron(np.eye(8), steps))
    plane = (spectrum(CX)[:, None] + spectrum(CZ)[None, :]).astype(np.float32)
    common = np.zeros((1120, 256))
    for name, value in (("rz", restrict_z), ("pz", prolong_z), ("fx", forward_x.reshape(256, 256)), ("ph", halo), ("sz", sine_z)):
        common[ROWS[name], : value.shape[1]] = value
    common[ROWS["kxz"]] = plane_xz.reshape(128, 2, 256).transpose(1, 0, 2).reshape(256, 256)
    along = np.concatenate([np.asarray(v, np.float64) for v in (gather, spread, edge_y)], axis=1)
    return (
        rounded(common),
        rounded(along),
        rounded(inverse_x.reshape(NBX, 32, 256)),
        plane,
        spectrum(CY).astype(np.float32),
    )


def turn(values, block):
    values = list(values)
    for bit in (4, 2, 1):
        low = (block & bit) == 0
        for first in range(8):
            if first & bit:
                continue
            second = first | bit
            one, two = values[first], values[second]
            values[first] = jnp.where(low, one, pltpu.roll(two, 16 * bit, 1))
            values[second] = jnp.where(low, pltpu.roll(one, 128 - 16 * bit, 1), two)
    return values


def kernel(
    forcing_hbm, start_hbm, class_ref, coef, eigen_y, common_hbm, along_hbm, ix_hbm, plane_hbm,
    out_ref, resid_ref,
    f, s, z, r, inner, kap, beta, base, diag, dinv, wx, wxb, wzl, wzh, wzb, wyl, wyh, wyb,
    halos, zsend, ysend, khalo, kzsend, kysend, yadd,
    common, along, ix, plane, invlam, fine, swap, wide_swap,
    va, vsend, xg, vb, vbsend,
    load_sem, halo_s, halo_r, kap_s, kap_r, z1_s, z1_r, x_s, x_r, z2_s, z2_r,
):
    ib, iy, iz = lax.axis_index("bx"), lax.axis_index("by"), lax.axis_index("bz")
    loads = [
        pltpu.make_async_copy(src, dst, load_sem.at[i])
        for i, (src, dst) in enumerate(
            [
                (start_hbm, s.at[0]), (forcing_hbm, f), (plane_hbm, plane),
                (common_hbm, common), (along_hbm.at[iy], along), (ix_hbm.at[ib], ix),
            ]
        )
    ]
    for load in loads:
        load.start()

    def x_peer(offset):
        return lax.rem(ib // 4 + offset[0], 4) * 4 + lax.rem(lax.rem(ib, 4) + offset[1], 4)

    def plane_peer(offset):
        return lax.rem(iy + offset[0], NBY), lax.rem(iz + offset[1], NBZ)

    barrier = pltpu.get_barrier_semaphore()
    for offset in OFFSETS:
        pl.semaphore_signal(barrier, inc=1, device_id={"bx": x_peer(offset)}, device_id_type=MESH)
    for offset in PLANE[::-1]:
        py, pz_ = plane_peer(offset)
        pl.semaphore_signal(barrier, inc=1, device_id={"by": py, "bz": pz_}, device_id_type=MESH)

    row = lax.broadcasted_iota(jnp.int32, (32, 128), 0)
    lane = lax.broadcasted_iota(jnp.int32, (32, 128), 1)
    spread_y = (lax.broadcasted_iota(jnp.int32, (32, 128), 1) // 4 == row).astype(F32).astype(BF16)
    tall = lax.broadcasted_iota(jnp.int32, (128, 32), 0) // 4
    spread_z = (tall == lax.broadcasted_iota(jnp.int32, (128, 32), 1)).astype(F32).astype(BF16)
    labels = class_ref[...].astype(F32).astype(BF16)
    labels = jnp.dot(labels, spread_y, preferred_element_type=F32).astype(BF16)
    labels = jnp.dot(spread_z, labels, preferred_element_type=F32)
    kappa = jnp.zeros((128, 128), F32)
    sigma = jnp.zeros((128, 128), F32)
    cubic = jnp.zeros((128, 128), F32)
    for index in range(16):
        hit = labels == float(index)
        kappa = jnp.where(hit, coef[0, index], kappa)
        sigma = jnp.where(hit, coef[1, index], sigma)
        cubic = jnp.where(hit, coef[2, index], cubic)
    kap[...] = kappa.reshape(4, 32, 128)
    base[...] = sigma.reshape(4, 32, 128)
    beta[...] = cubic.reshape(4, 32, 128)
    kysend[...] = jnp.transpose(pltpu.roll(kappa, 1, 1))[0:8]
    kzsend[0:4] = kap[:, 0, :]
    kzsend[4:8] = kap[:, 31, :]

    def pack(field, slot):
        wide = lax.broadcasted_iota(jnp.int32, (128, 128), 1)
        edge = jnp.zeros((128, 128), F32)
        for e in range(4):
            part = field[4 * e : 4 * e + 4].reshape(128, 128)
            edge = jnp.where(wide // 2 == e, pltpu.roll(part, 1 + 2 * e, 1), edge)
        ysend[slot] = jnp.transpose(edge)[0:8]
        zsend[slot, 0] = field[:, 0, :]
        zsend[slot, 1] = field[:, 31, :]

    xa, xb = lax.rem(ib + 15, NBX), lax.rem(ib + 1, NBX)
    ya, yb = lax.rem(iy + 3, NBY), lax.rem(iy + 1, NBY)
    za, zb = lax.rem(iz + 7, NBZ), lax.rem(iz + 1, NBZ)

    def remote(src, dst, send, recv, device):
        return pltpu.make_async_remote_copy(
            src_ref=src, dst_ref=dst, send_sem=send, recv_sem=recv, device_id=device, device_id_type=MESH
        )

    def halo(field, slot):
        to, ss, rs = halos.at[slot], halo_s.at[slot], halo_r.at[slot]
        return [
            remote(field.at[0], to.at[32:64], ss, rs, {"bx": xa}),
            remote(field.at[15], to.at[0:32], ss, rs, {"bx": xb}),
            remote(zsend.at[slot, 0], to.at[80:96], ss, rs, {"bz": za}),
            remote(zsend.at[slot, 1], to.at[64:80], ss, rs, {"bz": zb}),
            remote(ysend.at[slot], to.at[104:112], ss, rs, {"by": ya}),
            remote(ysend.at[slot], to.at[96:104], ss, rs, {"by": yb}),
        ]

    def halo_wait(slot):
        remote(halos.at[slot], halos.at[slot], halo_s.at[slot], halo_r.at[slot], {"bx": xa}).wait()

    loads[0].wait()
    pack(s.at[0], 0)
    kappa_copies = [
        remote(kap.at[0], khalo.at[32:64], kap_s.at[0], kap_r.at[0], {"bx": xa}),
        remote(kap.at[3], khalo.at[0:32], kap_s.at[0], kap_r.at[0], {"bx": xb}),
        remote(kzsend, khalo.at[72:80], kap_s.at[0], kap_r.at[0], {"bz": za}),
        remote(kzsend, khalo.at[64:72], kap_s.at[0], kap_r.at[0], {"bz": zb}),
        remote(kysend, khalo.at[88:96], kap_s.at[0], kap_r.at[0], {"by": ya}),
        remote(kysend, khalo.at[80:88], kap_s.at[0], kap_r.at[0], {"by": yb}),
    ]
    pl.semaphore_wait(barrier, len(OFFSETS) + len(PLANE))
    for copy in kappa_copies:
        copy.start()
    for copy in halo(s.at[0], 0):
        copy.start()

    zero = jnp.zeros((32, 128), F32)
    for e in range(4):
        k = kap[e]
        first, second, third = (row % 4 == 0), (row % 4 == 3), (lane % 4 == 0)
        zl = jnp.where(row == 0, zero, jnp.where(first, pltpu.roll(k, 1, 0) + k, k))
        zu = jnp.where(row == 31, zero, jnp.where(second, pltpu.roll(k, 31, 0) + k, k))
        yl = jnp.where(lane == 0, zero, jnp.where(third, pltpu.roll(k, 1, 1) + k, k))
        yu = jnp.where(lane == 127, zero, jnp.where(lane % 4 == 3, pltpu.roll(k, 127, 1) + k, k))
        wzl[e], wzh[e], wyl[e], wyh[e] = zl, zu, yl, yu
        base[e] = base[e] + ((zl + zu) + (yl + yu))
        for j in range(4):
            if j > 0:
                wx[4 * e + j] = k
            elif e > 0:
                wx[4 * e] = kap[e - 1] + k
    wx[0] = zero
    wx[16] = zero

    def inner_sum(field):
        def step(e, carry):
            zl, zu, yl, yu = wzl[e], wzh[e], wyl[e], wyh[e]
            for j in range(4):
                x = 4 * e + j
                v = field[x]
                total = zl * pltpu.roll(v, 1, 0) + zu * pltpu.roll(v, 31, 0)
                total = total + yl * pltpu.roll(v, 1, 1) + yu * pltpu.roll(v, 127, 1)
                total = total + wx[x] * field[lax.rem(x + 15, 16)]
                total = total + wx[x + 1] * field[lax.rem(x + 1, 16)]
                inner[x] = total
            return carry

        lax.fori_loop(0, 4, step, 0)

    inner_sum(s.at[0])

    kbar, sbar = coef[0, 0], coef[1, 0]
    for index in range(1, 16):
        kbar, sbar = kbar + coef[0, index], sbar + coef[1, index]
    kbar, sbar = kbar * 0.0625, sbar * 0.0625
    loads[2].wait()
    mode = iy * 64 + iz * 8
    for member in range(2):
        for pair in range(4):
            value = kbar * (plane[...] + eigen_y[mode + 2 * pair + member]) + sbar
            invlam[pl.ds(member * 128, 128), pl.ds(pair * 128, 128)] = 1.0 / value

    def inside(flag):
        return jnp.where(flag, 1.0, 0.0).astype(F32)

    x_in = (inside(ib > 0), inside(ib < NBX - 1))
    z_in = (inside(iz > 0), inside(iz < NBZ - 1))
    y_in = (inside(iy > 0), inside(iy < NBY - 1))
    remote(khalo, khalo, kap_s.at[0], kap_r.at[0], {"bx": xa}).wait()
    row8 = lax.broadcasted_iota(jnp.int32, (8, 128), 0)
    ends = []
    for side, e in ((0, 0), (1, 3)):
        weight = kap[e] + khalo[32 * side : 32 * side + 32] * x_in[side]
        wxb[side] = weight * x_in[side]
        ends.append(weight)
    low_y = jnp.transpose(khalo[80:88])[:, 0:1]
    high_y = jnp.transpose(khalo[88:96])[:, 1:2]
    wide = lax.broadcasted_iota(jnp.int32, (128, 128), 1)
    outer = jnp.where(wide == 0, y_in[0], jnp.where(wide == 127, y_in[1], 0.0))
    other = jnp.where(wide == 0, jnp.broadcast_to(low_y, (128, 128)), jnp.broadcast_to(high_y, (128, 128)))
    edge_y = (wide == 0) | (wide == 127)
    edge_y = jnp.where(edge_y, kap[...].reshape(128, 128) + other * outer, 0.0)
    wyb[...] = (edge_y * outer).reshape(4, 32, 128)
    base[...] = base[...] + edge_y.reshape(4, 32, 128)
    for e in range(4):
        low = jnp.where(row8 == 0, kap[e, 0:8, :] + khalo[68 + e : 69 + e, :] * z_in[0], 0.0)
        high = jnp.where(row8 == 7, kap[e, 24:32, :] + khalo[72 + e : 73 + e, :] * z_in[1], 0.0)
        wzb[0, e] = low * z_in[0]
        wzb[1, e] = high * z_in[1]
        base[e, 0:8, :] = base[e, 0:8, :] + low
        base[e, 24:32, :] = base[e, 24:32, :] + high
    for x in range(16):
        below = ends[0] if x == 0 else wx[x]
        above = ends[1] if x == 15 else wx[x + 1]
        total = base[x // 4] + (below + above)
        diag[x] = total

    def outer_sum(x_sides, z_sides, y_rows):
        inner[0] = inner[0] + wxb[0] * x_sides[0]
        inner[15] = inner[15] + wxb[1] * x_sides[1]
        columns = jnp.transpose(y_rows)
        wide = lax.broadcasted_iota(jnp.int32, (128, 128), 1)
        for e in range(4):
            low = jnp.broadcast_to(columns[:, e : e + 1], (128, 128))
            high = jnp.broadcast_to(columns[:, 4 + e : 5 + e], (128, 128))
            other = jnp.where(wide == 0, low, high).reshape(4, 32, 128)
            weight = wyb[e]
            for j in range(4):
                x = 4 * e + j
                inner[x] = inner[x] + weight * other[j]
                inner[x, 0:8, :] = inner[x, 0:8, :] + wzb[0, e] * z_sides[0][x : x + 1, :]
                inner[x, 24:32, :] = inner[x, 24:32, :] + wzb[1, e] * z_sides[1][x : x + 1, :]

    def arrived(slot):
        for e in range(4):
            yadd[slot, e : e + 1, :] = halos[slot, 96 + 2 * e : 97 + 2 * e, :]
            yadd[slot, 4 + e : 5 + e, :] = halos[slot, 105 + 2 * e : 106 + 2 * e, :]
        got = halos[slot, 0:96, :]
        return [got[0:32], got[32:64]], [got[64:80], got[80:96]], yadd[slot]

    def restricted(e, planes):
        one, two, three, four = planes
        for half, value in ((0, 3.0 * one + 2.0 * two + three), (1, two + 2.0 * three + 3.0 * four)):
            high = value.astype(BF16)
            at = pl.ds((2 * e + half) * 32, 32)
            fine[at, 0:128] = high
            fine[at, 128:256] = (value - high.astype(F32)).astype(BF16)

    def fused(field, store, x_sides, z_sides, y_rows, last):
        columns = jnp.transpose(y_rows)
        wide = lax.broadcasted_iota(jnp.int32, (128, 128), 1)
        for e in range(4):
            low = jnp.broadcast_to(columns[:, e : e + 1], (128, 128))
            high = jnp.broadcast_to(columns[:, 4 + e : 5 + e], (128, 128))
            other = jnp.where(wide == 0, low, high).reshape(4, 32, 128)
            planes = []
            for j in range(4):
                x = 4 * e + j
                v = field[x]
                total = wzl[e] * pltpu.roll(v, 1, 0) + wzh[e] * pltpu.roll(v, 31, 0)
                total = total + wyl[e] * pltpu.roll(v, 1, 1) + wyh[e] * pltpu.roll(v, 127, 1)
                total = total + wyb[e] * other[j]
                total = total + (wxb[0] * x_sides[0] if x == 0 else wx[x] * field[x - 1])
                total = total + (wxb[1] * x_sides[1] if x == 15 else wx[x + 1] * field[x + 1])
                low_z = total[0:8] + wzb[0, e] * z_sides[0][x : x + 1, :]
                high_z = total[24:32] + wzb[1, e] * z_sides[1][x : x + 1, :]
                total = jnp.concatenate([low_z, total[8:24], high_z], axis=0)
                value = (f[x] - (diag[x] * v - total)) - beta[e] * v * v * v
                store[x] = value
                planes.append(value)
            if not last:
                restricted(e, planes)

    def residual(field, store):
        for e in range(4):
            cube = beta[e]
            planes = []
            for j in range(4):
                x = 4 * e + j
                v = field[x]
                value = (f[x] - (diag[x] * v - inner[x])) - cube * v * v * v
                store[x] = value
                planes.append(value)
            restricted(e, planes)

    block = lax.broadcasted_iota(jnp.int32, (8, 128), 1) // 16
    loads[1].wait()
    for load in loads[3:]:
        load.wait()
    halo_wait(0)
    outer_sum(*arrived(0))
    residual(s.at[0], r)
    rz, pz, fx, ph = (common.at[ROWS[name]] for name in ("rz", "pz", "fx", "ph"))
    sz = common.at[ROWS["sz"], 0:128]
    kxz = common.at[ROWS["kxz"]]
    gy, sp, ey = along.at[0:256], along.at[256:512], along.at[512:528]
    lane8 = lax.broadcasted_iota(jnp.int32, (8, 128), 1)
    me = iy * NBZ + iz

    for cycle in range(CYCLES):
        value = jnp.dot(rz[...], fine[...], preferred_element_type=F32)
        value = ((value[:, 0:128] + value[:, 128:256]) * (1.0 / 36.0)).astype(BF16)
        value = jnp.concatenate([value, value], axis=1)
        value = lax.dot_general(gy[...], value, (((1,), (1,)), ((), ())), preferred_element_type=F32)
        vsend[cycle] = value.reshape(32, 8, 128).astype(BF16)

        def forward(offset):
            py, pz_ = plane_peer(offset)
            return remote(
                vsend.at[cycle, py * NBZ + pz_], va.at[cycle, me], z1_s.at[cycle], z1_r.at[cycle], {"by": py, "bz": pz_}
            )

        for o in PLANE:
            forward(o).start()
        va[cycle, me] = vsend[cycle, me]

        smooth = z.at[cycle]
        if cycle == 0:
            dinv[...] = DAMPING / diag[...]
        smooth[...] = r[...] * dinv[...]
        pack(smooth, 2 * cycle + 1)
        for copy in halo(smooth, 2 * cycle + 1):
            copy.start()
        inner_sum(smooth)
        some = va.at[cycle, pl.ds(0, 31)]
        forward_all = remote(some, some, z1_s.at[cycle], z1_r.at[cycle], {"bz": zb})
        forward_all.wait_recv()
        parts = []
        for i in range(8):
            one, two, three, four = (va[cycle, 8 * j + i].astype(F32) for j in range(4))
            parts.append((one + two) + (three + four))
        value = jnp.concatenate(turn(parts, block), axis=0).astype(BF16)
        swap[...] = jnp.dot(value, sz[...], preferred_element_type=F32)
        value = jnp.concatenate([swap[pl.ds(m, 8, stride=8), :] for m in range(8)], axis=0)
        xg[cycle, ib] = value.reshape(4, 16, 128).astype(BF16)
        for o in OFFSETS:
            remote(xg.at[cycle, ib], xg.at[cycle, ib], x_s.at[cycle], x_r.at[cycle], {"bx": x_peer(o)}).start()
        forward_all.wait_send()

        final = cycle == CYCLES - 1
        after = out_ref if final else s.at[cycle + 1]
        halo_wait(2 * cycle + 1)
        outer_sum(*arrived(2 * cycle + 1))
        after[...] = s[cycle] + ((2.0 - DAMPING) * smooth[...] + dinv[...] * inner[...])
        pack(after, 2 * cycle + 2)
        for copy in halo(after, 2 * cycle + 2):
            copy.start()
        some = xg.at[cycle, pl.ds(0, 15)]
        x_all = remote(some, some, x_s.at[cycle], x_r.at[cycle], {"bx": xa})
        x_all.wait_recv()
        parts = []
        for half in range(2):
            value = jnp.concatenate(
                [xg[cycle, :, 2 * half + i, :, :].reshape(256, 128) for i in range(2)], axis=1
            )
            value = jnp.dot(fx[...], value, preferred_element_type=F32)
            value = (value * invlam[:, 256 * half : 256 * half + 256]).astype(BF16)
            value = jnp.dot(ix[...], value, preferred_element_type=F32)
            parts += [value[:, 0:128], value[:, 128:256]]
        value = jnp.concatenate(parts, axis=0).astype(BF16)
        wide_swap[...] = jnp.dot(value, sz[...], preferred_element_type=F32)
        lines = [wide_swap[pl.ds(i, 8, stride=16), :] for i in range(10)]
        low = high = none = jnp.zeros((8, 128), F32)
        for i in range(8):
            low = jnp.where(lane8 % 16 == i, pltpu.roll(lines[i], 1 + i, 1), low)
            high = jnp.where(lane8 % 16 == i, pltpu.roll(lines[i], 112 + i, 1), high)
        own = turn(lines[0:8], block)
        beyond = turn([lines[8], lines[9], low, high, none, none, none, none], block)
        for i in range(8):
            vbsend[cycle, i, 0] = own[i].astype(BF16)
            vbsend[cycle, i, 1] = beyond[i].astype(BF16)

        def backward(offset):
            py, pz_ = plane_peer(offset)
            return remote(
                vbsend.at[cycle, pz_], vb.at[cycle, me], z2_s.at[cycle], z2_r.at[cycle], {"by": py, "bz": pz_}
            )

        for o in PLANE:
            backward(o).start()
        vb[cycle, me] = vbsend[cycle, iz]
        x_all.wait_send()
        halo_wait(2 * cycle + 2)
        x_sides, z_sides, y_rows = arrived(2 * cycle + 2)
        some = vb.at[cycle, pl.ds(0, 31)]
        back_all = remote(some, some, z2_s.at[cycle], z2_r.at[cycle], {"bz": zb})
        back_all.wait_recv()

        own = vb[cycle, :, 0].astype(F32).reshape(CY, 128).astype(BF16)
        beyond = vb[cycle, :, 1].astype(F32).reshape(CY, 128).astype(BF16)
        value = lax.dot_general(
            jnp.concatenate([own, beyond], axis=1), sp[...], (((0,), (0,)), ((), ())), preferred_element_type=F32
        )
        value = value[:, 0:128] + value[:, 128:256]
        high = value.astype(BF16)
        low = (value - high.astype(F32)).astype(BF16)
        value = jnp.dot(pz[...], jnp.concatenate([high[0:128], low[0:128]], axis=0), preferred_element_type=F32)
        value = (value * (1.0 / 3.0)).reshape(8, 32, 128)
        outside = jnp.dot(ph[...], jnp.concatenate([high[128:256], low[128:256]], axis=0), preferred_element_type=F32)
        outside = outside * (1.0 / 3.0)
        edge = jnp.dot(ey[...], own, preferred_element_type=F32)
        high = edge.astype(BF16)
        low = (edge - high.astype(F32)).astype(BF16)
        edge = jnp.concatenate([high, low], axis=0)
        edge = [jnp.dot(edge, kxz[128 * i : 128 * i + 128, :], preferred_element_type=F32) for i in range(2)]
        edge = [(part[0:8] + part[16:24]) * (1.0 / 9.0) for part in edge]
        for e in range(4):
            one, two = value[2 * e], value[2 * e + 1]
            mixed = (one, one * (2.0 / 3.0) + two * (1.0 / 3.0), one * (1.0 / 3.0) + two * (2.0 / 3.0), two)
            for j in range(4):
                after[4 * e + j] = after[4 * e + j] + mixed[j]
            part = edge[e // 2][:, 128 * (e % 2) : 128 * (e % 2) + 128]
            yadd[5, e : e + 1, :] = part[0:1]
            yadd[5, 4 + e : 5 + e, :] = part[1:2]
        fused(
            after,
            resid_ref if final else r,
            [x_sides[0] + outside[0:32], x_sides[1] + outside[32:64]],
            [z_sides[0] + outside[64:80], z_sides[1] + outside[80:96]],
            y_rows + yadd[5],
            final,
        )
        back_all.wait_send()


def body(forcing, start, element_class_index, class_coef):
    consts = [jnp.asarray(t) for t in tables()]
    eigen_y = consts.pop()
    full, brick = (16, 32, 128), (4, 32, 128)
    vmem = pltpu.VMEM
    dma = pltpu.SemaphoreType.DMA
    scratch = (
        [vmem(full, F32), vmem((2,) + full, F32), vmem((2,) + full, F32), vmem(full, F32), vmem(full, F32)]
        + [vmem(brick, F32)] * 3
        + [vmem(full, F32)] * 2
        + [vmem((17, 32, 128), F32), vmem((2, 32, 128), F32)]
        + [vmem(brick, F32)] * 2
        + [vmem((2, 4, 8, 128), F32)]
        + [vmem(brick, F32)] * 3
        + [vmem((5, 112, 128), F32), vmem((5, 2, 16, 128), F32), vmem((5, 8, 128), F32)]
        + [vmem((96, 128), F32), vmem((8, 128), F32), vmem((8, 128), F32), vmem((6, 8, 128), F32)]
        + [vmem((1120, 256), BF16), vmem((528, 256), BF16), vmem((32, 256), BF16)]
        + [vmem((128, 128), F32), vmem((256, 512), F32)]
        + [vmem((256, 256), BF16), vmem((64, 128), F32), vmem((128, 128), F32)]
        + [vmem((2, 32, 8, 128), BF16), vmem((2, 32, 8, 128), BF16), vmem((2, 16, 4, 16, 128), BF16)]
        + [vmem((2, 32, 2, 8, 128), BF16), vmem((2, 8, 2, 8, 128), BF16)]
        + [dma((6,)), dma((5,)), dma((5,)), dma((1,)), dma((1,))]
        + [dma((2,))] * 6
    )
    anywhere = pl.BlockSpec(memory_space=pl.ANY)
    scalar = pl.BlockSpec(memory_space=pltpu.SMEM)
    shape = pltpu.VMEM(full, F32)
    return pl.pallas_call(
        kernel,
        out_shape=(shape, shape),
        in_specs=[anywhere, anywhere, pl.BlockSpec(memory_space=pltpu.VMEM), scalar, scalar] + [anywhere] * 4,
        out_specs=(pl.BlockSpec(memory_space=pltpu.VMEM),) * 2,
        scratch_shapes=scratch,
        compiler_params=pltpu.CompilerParams(collective_id=0, has_side_effects=True),
        name="cycles",
    )(forcing, start, element_class_index.reshape(32, 32), class_coef, eigen_y, *consts)


def solution(mesh):
    spec = P("bx", "bz", "by")
    return jax.shard_map(
        body, mesh=mesh, in_specs=(spec, spec, spec, P()), out_specs=(spec, spec), check_vma=False
    )
```

```python
import math

import jax
import jax.numpy as jnp
import numpy as np
from jax import lax
from jax.experimental import pallas as pl
from jax.experimental.pallas import tpu as pltpu
from jax.sharding import PartitionSpec as P

CYCLES = 2
DAMPING = 0.6666666666666666
NBX, NBY, NBZ = 16, 4, 8
CX, CZ, CY = 128, 128, 256
F32, BF16 = jnp.float32, jnp.bfloat16
MESH = pl.DeviceIdType.MESH
OFFSETS = sorted(
    ((a, b) for a in range(4) for b in range(4) if (a, b) != (0, 0)),
    key=lambda o: -(min(o[0], 4 - o[0]) + 2 * min(o[1], 4 - o[1])),
)


PLANE = [(a, b) for b in (4, 3, 5, 2, 6, 1, 7, 0) for a in (2, 3, 1, 0) if (a, b) != (0, 0)]


ROWS = {
    "rz": slice(0, 128), "pz": slice(128, 384), "fx": slice(384, 640),
    "ph": slice(640, 736), "kxz": slice(736, 992), "sz": slice(992, 1120),
}


def rounded(value):
    return np.asarray(value, dtype=np.float64).astype(np.float32).astype(jnp.bfloat16)


def sine(count):
    index = np.arange(1, count + 1, dtype=np.float64)
    table = np.sin(np.outer(index, index) * (math.pi / (count + 1))) * math.sqrt(2.0 / (count + 1))
    return rounded(table).astype(np.float64)


def spectrum(count):
    return 2.0 - 2.0 * np.cos(np.arange(1, count + 1) * (math.pi / (count + 1)))


def split(value):
    high = rounded(value)
    return high, rounded(value - high.astype(np.float64))


def tables():
    sine_x, sine_z, sine_y = sine(CX), sine(CZ), sine(CY)
    steps = np.array([[3.0, 2.0, 1.0, 0.0], [0.0, 1.0, 2.0, 3.0]])
    restrict_z = np.kron(np.eye(64), steps)
    prolong_z = np.concatenate([restrict_z.T, restrict_z.T], axis=1)
    blocks = sine_x.reshape(CX, NBX, 8)
    forward_x = np.zeros((2, CX, NBX, 2, 8))
    inverse_x = np.zeros((NBX, 2, 16, 2, CX))
    for member in range(2):
        forward_x[member, :, :, member, :] = blocks
        inverse_x[:, member, :8, member, :] = sine_x.reshape(NBX, 8, CX)
        inverse_x[1:, member, 8, member, :] = sine_x[7:-1:8]
        inverse_x[:-1, member, 9, member, :] = sine_x[8::8]
    along_y = np.kron(np.eye(CY // 2), steps)
    spread = (sine_y @ along_y / 3.0).reshape(CY, NBY, 128).transpose(1, 0, 2)
    spread = np.concatenate(split(spread), axis=2)
    gather = (sine_y.reshape(CY, NBY, 64).transpose(1, 0, 2) @ np.kron(np.eye(32), steps)) / 6.0
    gather = np.concatenate(split(gather), axis=2)
    edge_y = np.zeros((NBY, 16, CY))
    edge_y[1:, 0] = sine_y[63:-1:64]
    edge_y[:-1, 1] = sine_y[64::64]
    halo = np.zeros((96, 128))
    for side in range(2):
        halo[32 * side : 32 * side + 32, 16 * side : 16 * side + 16] = np.kron(np.eye(8), steps).T
        halo[64 + 16 * side : 80 + 16 * side, 32 + 16 * side : 40 + 16 * side] = np.kron(np.eye(4), steps).T
    halo = np.concatenate([halo, halo], axis=1)
    plane_xz = np.kron(np.kron(np.eye(4), steps), np.kron(np.eye(8), steps))
    plane = (spectrum(CX)[:, None] + spectrum(CZ)[None, :]).astype(np.float32)
    common = np.zeros((1120, 256))
    for name, value in (("rz", restrict_z), ("pz", prolong_z), ("fx", forward_x.reshape(256, 256)), ("ph", halo), ("sz", sine_z)):
        common[ROWS[name], : value.shape[1]] = value
    common[ROWS["kxz"]] = plane_xz.reshape(128, 2, 256).transpose(1, 0, 2).reshape(256, 256)
    along = np.concatenate([np.asarray(v, np.float64) for v in (gather, spread, edge_y)], axis=1)
    return (
        rounded(common),
        rounded(along),
        rounded(inverse_x.reshape(NBX, 32, 256)),
        plane,
        spectrum(CY).astype(np.float32),
    )


def turn(values, block):
    values = list(values)
    for bit in (4, 2, 1):
        low = (block & bit) == 0
        for first in range(8):
            if first & bit:
                continue
            second = first | bit
            one, two = values[first], values[second]
            values[first] = jnp.where(low, one, pltpu.roll(two, 16 * bit, 1))
            values[second] = jnp.where(low, pltpu.roll(one, 128 - 16 * bit, 1), two)
    return values


def kernel(
    forcing_hbm, start_hbm, class_hbm, coef_hbm, eigen_hbm, common_hbm, along_hbm, ix_hbm, plane_hbm,
    out_ref, resid_ref,
    f, s, z, r, inner, kap, beta, base, diag, dinv, wx, wxb, wzl, wzh, wzb, wyl, wyh, wyb,
    class_ref, coef, eigen_y, halos, zsend, ysend, khalo, kzsend, kysend, yadd,
    common, along, ix, plane, invlam, fine, swap, wide_swap,
    va, vsend, xg, vb, vbsend,
    load_sem, halo_s, halo_r, kap_s, kap_r, z1_s, z1_r, x_s, x_r, z2_s, z2_r,
):
    ib, iy, iz = lax.axis_index("bx"), lax.axis_index("by"), lax.axis_index("bz")
    loads = [
        pltpu.make_async_copy(src, dst, load_sem.at[i])
        for i, (src, dst) in enumerate(
            [
                (start_hbm, s.at[0]), (class_hbm, class_ref), (coef_hbm, coef), (eigen_hbm, eigen_y),
                (plane_hbm, plane), (forcing_hbm, f),
                (common_hbm, common), (along_hbm.at[iy], along), (ix_hbm.at[ib], ix),
            ]
        )
    ]
    def x_peer(offset):
        return lax.rem(ib // 4 + offset[0], 4) * 4 + lax.rem(lax.rem(ib, 4) + offset[1], 4)

    def plane_peer(offset):
        return lax.rem(iy + offset[0], NBY), lax.rem(iz + offset[1], NBZ)

    barrier = pltpu.get_barrier_semaphore()
    for offset in OFFSETS:
        pl.semaphore_signal(barrier, inc=1, device_id={"bx": x_peer(offset)}, device_id_type=MESH)
    for offset in PLANE[::-1]:
        py, pz_ = plane_peer(offset)
        pl.semaphore_signal(barrier, inc=1, device_id={"by": py, "bz": pz_}, device_id_type=MESH)

    for load in loads:
        load.start()

    row = lax.broadcasted_iota(jnp.int32, (32, 128), 0)
    lane = lax.broadcasted_iota(jnp.int32, (32, 128), 1)
    spread_y = (lax.broadcasted_iota(jnp.int32, (32, 128), 1) // 4 == row).astype(F32).astype(BF16)
    tall = lax.broadcasted_iota(jnp.int32, (128, 32), 0) // 4
    spread_z = (tall == lax.broadcasted_iota(jnp.int32, (128, 32), 1)).astype(F32).astype(BF16)
    loads[1].wait()
    loads[2].wait()
    labels = class_ref[...].astype(F32).astype(BF16)
    labels = jnp.dot(labels, spread_y, preferred_element_type=F32).astype(BF16)
    labels = jnp.dot(spread_z, labels, preferred_element_type=F32)
    kappa = jnp.zeros((128, 128), F32)
    sigma = jnp.zeros((128, 128), F32)
    cubic = jnp.zeros((128, 128), F32)
    for index in range(16):
        hit = labels == float(index)
        kappa = jnp.where(hit, coef[0, index], kappa)
        sigma = jnp.where(hit, coef[1, index], sigma)
        cubic = jnp.where(hit, coef[2, index], cubic)
    kap[...] = kappa.reshape(4, 32, 128)
    base[...] = sigma.reshape(4, 32, 128)
    beta[...] = cubic.reshape(4, 32, 128)
    kysend[...] = jnp.transpose(pltpu.roll(kappa, 1, 1))[0:8]
    kzsend[0:4] = kap[:, 0, :]
    kzsend[4:8] = kap[:, 31, :]

    def pack(field, slot):
        wide = lax.broadcasted_iota(jnp.int32, (128, 128), 1)
        edge = jnp.zeros((128, 128), F32)
        for e in range(4):
            part = field[4 * e : 4 * e + 4].reshape(128, 128)
            edge = jnp.where(wide // 2 == e, pltpu.roll(part, 1 + 2 * e, 1), edge)
        ysend[slot] = jnp.transpose(edge)[0:8]
        zsend[slot, 0] = field[:, 0, :]
        zsend[slot, 1] = field[:, 31, :]

    xa, xb = lax.rem(ib + 15, NBX), lax.rem(ib + 1, NBX)
    ya, yb = lax.rem(iy + 3, NBY), lax.rem(iy + 1, NBY)
    za, zb = lax.rem(iz + 7, NBZ), lax.rem(iz + 1, NBZ)

    def remote(src, dst, send, recv, device):
        return pltpu.make_async_remote_copy(
            src_ref=src, dst_ref=dst, send_sem=send, recv_sem=recv, device_id=device, device_id_type=MESH
        )

    def halo(field, slot):
        to, ss, rs = halos.at[slot], halo_s.at[slot], halo_r.at[slot]
        return [
            remote(field.at[0], to.at[32:64], ss, rs, {"bx": xa}),
            remote(field.at[15], to.at[0:32], ss, rs, {"bx": xb}),
            remote(zsend.at[slot, 0], to.at[80:96], ss, rs, {"bz": za}),
            remote(zsend.at[slot, 1], to.at[64:80], ss, rs, {"bz": zb}),
            remote(ysend.at[slot], to.at[104:112], ss, rs, {"by": ya}),
            remote(ysend.at[slot], to.at[96:104], ss, rs, {"by": yb}),
        ]

    def halo_wait(slot):
        remote(halos.at[slot], halos.at[slot], halo_s.at[slot], halo_r.at[slot], {"bx": xa}).wait()

    loads[0].wait()
    pack(s.at[0], 0)
    kappa_copies = [
        remote(kap.at[0], khalo.at[32:64], kap_s.at[0], kap_r.at[0], {"bx": xa}),
        remote(kap.at[3], khalo.at[0:32], kap_s.at[0], kap_r.at[0], {"bx": xb}),
        remote(kzsend, khalo.at[72:80], kap_s.at[0], kap_r.at[0], {"bz": za}),
        remote(kzsend, khalo.at[64:72], kap_s.at[0], kap_r.at[0], {"bz": zb}),
        remote(kysend, khalo.at[88:96], kap_s.at[0], kap_r.at[0], {"by": ya}),
        remote(kysend, khalo.at[80:88], kap_s.at[0], kap_r.at[0], {"by": yb}),
    ]
    pl.semaphore_wait(barrier, len(OFFSETS) + len(PLANE))
    for copy in kappa_copies:
        copy.start()
    for copy in halo(s.at[0], 0):
        copy.start()

    zero = jnp.zeros((32, 128), F32)
    for e in range(4):
        k = kap[e]
        first, second, third = (row % 4 == 0), (row % 4 == 3), (lane % 4 == 0)
        zl = jnp.where(row == 0, zero, jnp.where(first, pltpu.roll(k, 1, 0) + k, k))
        zu = jnp.where(row == 31, zero, jnp.where(second, pltpu.roll(k, 31, 0) + k, k))
        yl = jnp.where(lane == 0, zero, jnp.where(third, pltpu.roll(k, 1, 1) + k, k))
        yu = jnp.where(lane == 127, zero, jnp.where(lane % 4 == 3, pltpu.roll(k, 127, 1) + k, k))
        wzl[e], wzh[e], wyl[e], wyh[e] = zl, zu, yl, yu
        base[e] = base[e] + ((zl + zu) + (yl + yu))
        for j in range(4):
            if j > 0:
                wx[4 * e + j] = k
            elif e > 0:
                wx[4 * e] = kap[e - 1] + k
    wx[0] = zero
    wx[16] = zero

    def inner_sum(field):
        def step(e, carry):
            zl, zu, yl, yu = wzl[e], wzh[e], wyl[e], wyh[e]
            for j in range(4):
                x = 4 * e + j
                v = field[x]
                total = zl * pltpu.roll(v, 1, 0) + zu * pltpu.roll(v, 31, 0)
                total = total + yl * pltpu.roll(v, 1, 1) + yu * pltpu.roll(v, 127, 1)
                total = total + wx[x] * field[lax.rem(x + 15, 16)]
                total = total + wx[x + 1] * field[lax.rem(x + 1, 16)]
                inner[x] = total
            return carry

        lax.fori_loop(0, 4, step, 0)

    inner_sum(s.at[0])

    kbar, sbar = coef[0, 0], coef[1, 0]
    for index in range(1, 16):
        kbar, sbar = kbar + coef[0, index], sbar + coef[1, index]
    kbar, sbar = kbar * 0.0625, sbar * 0.0625
    loads[3].wait()
    loads[4].wait()
    mode = iy * 64 + iz * 8
    for member in range(2):
        for pair in range(4):
            value = kbar * (plane[...] + eigen_y[mode + 2 * pair + member]) + sbar
            invlam[pl.ds(member * 128, 128), pl.ds(pair * 128, 128)] = 1.0 / value

    def inside(flag):
        return jnp.where(flag, 1.0, 0.0).astype(F32)

    x_in = (inside(ib > 0), inside(ib < NBX - 1))
    z_in = (inside(iz > 0), inside(iz < NBZ - 1))
    y_in = (inside(iy > 0), inside(iy < NBY - 1))
    remote(khalo, khalo, kap_s.at[0], kap_r.at[0], {"bx": xa}).wait()
    row8 = lax.broadcasted_iota(jnp.int32, (8, 128), 0)
    ends = []
    for side, e in ((0, 0), (1, 3)):
        weight = kap[e] + khalo[32 * side : 32 * side + 32] * x_in[side]
        wxb[side] = weight * x_in[side]
        ends.append(weight)
    low_y = jnp.transpose(khalo[80:88])[:, 0:1]
    high_y = jnp.transpose(khalo[88:96])[:, 1:2]
    wide = lax.broadcasted_iota(jnp.int32, (128, 128), 1)
    outer = jnp.where(wide == 0, y_in[0], jnp.where(wide == 127, y_in[1], 0.0))
    other = jnp.where(wide == 0, jnp.broadcast_to(low_y, (128, 128)), jnp.broadcast_to(high_y, (128, 128)))
    edge_y = (wide == 0) | (wide == 127)
    edge_y = jnp.where(edge_y, kap[...].reshape(128, 128) + other * outer, 0.0)
    wyb[...] = (edge_y * outer).reshape(4, 32, 128)
    base[...] = base[...] + edge_y.reshape(4, 32, 128)
    for e in range(4):
        low = jnp.where(row8 == 0, kap[e, 0:8, :] + khalo[68 + e : 69 + e, :] * z_in[0], 0.0)
        high = jnp.where(row8 == 7, kap[e, 24:32, :] + khalo[72 + e : 73 + e, :] * z_in[1], 0.0)
        wzb[0, e] = low * z_in[0]
        wzb[1, e] = high * z_in[1]
        base[e, 0:8, :] = base[e, 0:8, :] + low
        base[e, 24:32, :] = base[e, 24:32, :] + high
    for x in range(16):
        below = ends[0] if x == 0 else wx[x]
        above = ends[1] if x == 15 else wx[x + 1]
        total = base[x // 4] + (below + above)
        diag[x] = total

    def outer_sum(x_sides, z_sides, y_rows):
        inner[0] = inner[0] + wxb[0] * x_sides[0]
        inner[15] = inner[15] + wxb[1] * x_sides[1]
        columns = jnp.transpose(y_rows)
        wide = lax.broadcasted_iota(jnp.int32, (128, 128), 1)
        for e in range(4):
            low = jnp.broadcast_to(columns[:, e : e + 1], (128, 128))
            high = jnp.broadcast_to(columns[:, 4 + e : 5 + e], (128, 128))
            other = jnp.where(wide == 0, low, high).reshape(4, 32, 128)
            weight = wyb[e]
            for j in range(4):
                x = 4 * e + j
                inner[x] = inner[x] + weight * other[j]
                inner[x, 0:8, :] = inner[x, 0:8, :] + wzb[0, e] * z_sides[0][x : x + 1, :]
                inner[x, 24:32, :] = inner[x, 24:32, :] + wzb[1, e] * z_sides[1][x : x + 1, :]

    def arrived(slot):
        for e in range(4):
            yadd[slot, e : e + 1, :] = halos[slot, 96 + 2 * e : 97 + 2 * e, :]
            yadd[slot, 4 + e : 5 + e, :] = halos[slot, 105 + 2 * e : 106 + 2 * e, :]
        got = halos[slot, 0:96, :]
        return [got[0:32], got[32:64]], [got[64:80], got[80:96]], yadd[slot]

    def restricted(e, planes):
        one, two, three, four = planes
        for half, value in ((0, 3.0 * one + 2.0 * two + three), (1, two + 2.0 * three + 3.0 * four)):
            high = value.astype(BF16)
            at = pl.ds((2 * e + half) * 32, 32)
            fine[at, 0:128] = high
            fine[at, 128:256] = (value - high.astype(F32)).astype(BF16)

    def fused(field, store, x_sides, z_sides, y_rows, last):
        columns = jnp.transpose(y_rows)
        wide = lax.broadcasted_iota(jnp.int32, (128, 128), 1)
        for e in range(4):
            low = jnp.broadcast_to(columns[:, e : e + 1], (128, 128))
            high = jnp.broadcast_to(columns[:, 4 + e : 5 + e], (128, 128))
            other = jnp.where(wide == 0, low, high).reshape(4, 32, 128)
            planes = []
            for j in range(4):
                x = 4 * e + j
                v = field[x]
                total = wzl[e] * pltpu.roll(v, 1, 0) + wzh[e] * pltpu.roll(v, 31, 0)
                total = total + wyl[e] * pltpu.roll(v, 1, 1) + wyh[e] * pltpu.roll(v, 127, 1)
                total = total + wyb[e] * other[j]
                total = total + (wxb[0] * x_sides[0] if x == 0 else wx[x] * field[x - 1])
                total = total + (wxb[1] * x_sides[1] if x == 15 else wx[x + 1] * field[x + 1])
                low_z = total[0:8] + wzb[0, e] * z_sides[0][x : x + 1, :]
                high_z = total[24:32] + wzb[1, e] * z_sides[1][x : x + 1, :]
                total = jnp.concatenate([low_z, total[8:24], high_z], axis=0)
                value = (f[x] - (diag[x] * v - total)) - beta[e] * v * v * v
                store[x] = value
                planes.append(value)
            if not last:
                restricted(e, planes)

    def residual(field, store):
        for e in range(4):
            cube = beta[e]
            planes = []
            for j in range(4):
                x = 4 * e + j
                v = field[x]
                value = (f[x] - (diag[x] * v - inner[x])) - cube * v * v * v
                store[x] = value
                planes.append(value)
            restricted(e, planes)

    block = lax.broadcasted_iota(jnp.int32, (8, 128), 1) // 16
    for load in loads[5:]:
        load.wait()
    halo_wait(0)
    outer_sum(*arrived(0))
    residual(s.at[0], r)
    rz, pz, fx, ph = (common.at[ROWS[name]] for name in ("rz", "pz", "fx", "ph"))
    sz = common.at[ROWS["sz"], 0:128]
    kxz = common.at[ROWS["kxz"]]
    gy, sp, ey = along.at[0:256], along.at[256:512], along.at[512:528]
    lane8 = lax.broadcasted_iota(jnp.int32, (8, 128), 1)
    me = iy * NBZ + iz

    for cycle in range(CYCLES):
        value = jnp.dot(rz[...], fine[...], preferred_element_type=F32)
        value = ((value[:, 0:128] + value[:, 128:256]) * (1.0 / 36.0)).astype(BF16)
        value = jnp.concatenate([value, value], axis=1)
        value = lax.dot_general(gy[...], value, (((1,), (1,)), ((), ())), preferred_element_type=F32)
        vsend[cycle] = value.reshape(32, 8, 128).astype(BF16)

        def forward(offset):
            py, pz_ = plane_peer(offset)
            return remote(
                vsend.at[cycle, py * NBZ + pz_], va.at[cycle, me], z1_s.at[cycle], z1_r.at[cycle], {"by": py, "bz": pz_}
            )

        for o in PLANE:
            forward(o).start()
        va[cycle, me] = vsend[cycle, me]

        smooth = z.at[cycle]
        if cycle == 0:
            dinv[...] = DAMPING / diag[...]
        smooth[...] = r[...] * dinv[...]
        pack(smooth, 2 * cycle + 1)
        for copy in halo(smooth, 2 * cycle + 1):
            copy.start()
        inner_sum(smooth)
        some = va.at[cycle, pl.ds(0, 31)]
        forward_all = remote(some, some, z1_s.at[cycle], z1_r.at[cycle], {"bz": zb})
        forward_all.wait_recv()
        parts = []
        for i in range(8):
            one, two, three, four = (va[cycle, 8 * j + i].astype(F32) for j in range(4))
            parts.append((one + two) + (three + four))
        value = jnp.concatenate(turn(parts, block), axis=0).astype(BF16)
        swap[...] = jnp.dot(value, sz[...], preferred_element_type=F32)
        value = jnp.concatenate([swap[pl.ds(m, 8, stride=8), :] for m in range(8)], axis=0)
        xg[cycle, ib] = value.reshape(4, 16, 128).astype(BF16)
        for o in OFFSETS:
            remote(xg.at[cycle, ib], xg.at[cycle, ib], x_s.at[cycle], x_r.at[cycle], {"bx": x_peer(o)}).start()
        forward_all.wait_send()

        final = cycle == CYCLES - 1
        after = out_ref if final else s.at[cycle + 1]
        halo_wait(2 * cycle + 1)
        outer_sum(*arrived(2 * cycle + 1))
        after[...] = s[cycle] + ((2.0 - DAMPING) * smooth[...] + dinv[...] * inner[...])
        pack(after, 2 * cycle + 2)
        some = xg.at[cycle, pl.ds(0, 15)]
        x_all = remote(some, some, x_s.at[cycle], x_r.at[cycle], {"bx": xa})
        x_all.wait_recv()
        parts = []
        for half in range(2):
            value = jnp.concatenate(
                [xg[cycle, :, 2 * half + i, :, :].reshape(256, 128) for i in range(2)], axis=1
            )
            value = jnp.dot(fx[...], value, preferred_element_type=F32)
            value = (value * invlam[:, 256 * half : 256 * half + 256]).astype(BF16)
            value = jnp.dot(ix[...], value, preferred_element_type=F32)
            parts += [value[:, 0:128], value[:, 128:256]]
        value = jnp.concatenate(parts, axis=0).astype(BF16)
        wide_swap[...] = jnp.dot(value, sz[...], preferred_element_type=F32)
        lines = [wide_swap[pl.ds(i, 8, stride=16), :] for i in range(10)]
        low = high = none = jnp.zeros((8, 128), F32)
        for i in range(8):
            low = jnp.where(lane8 % 16 == i, pltpu.roll(lines[i], 1 + i, 1), low)
            high = jnp.where(lane8 % 16 == i, pltpu.roll(lines[i], 112 + i, 1), high)
        own = turn(lines[0:8], block)
        beyond = turn([lines[8], lines[9], low, high, none, none, none, none], block)
        for i in range(8):
            vbsend[cycle, i, 0] = own[i].astype(BF16)
            vbsend[cycle, i, 1] = beyond[i].astype(BF16)

        def backward(offset):
            py, pz_ = plane_peer(offset)
            return remote(
                vbsend.at[cycle, pz_], vb.at[cycle, me], z2_s.at[cycle], z2_r.at[cycle], {"by": py, "bz": pz_}
            )

        for o in PLANE:
            backward(o).start()
        for copy in halo(after, 2 * cycle + 2):
            copy.start()
        vb[cycle, me] = vbsend[cycle, iz]
        x_all.wait_send()
        halo_wait(2 * cycle + 2)
        x_sides, z_sides, y_rows = arrived(2 * cycle + 2)
        some = vb.at[cycle, pl.ds(0, 31)]
        back_all = remote(some, some, z2_s.at[cycle], z2_r.at[cycle], {"bz": zb})
        back_all.wait_recv()

        own = vb[cycle, :, 0].astype(F32).reshape(CY, 128).astype(BF16)
        beyond = vb[cycle, :, 1].astype(F32).reshape(CY, 128).astype(BF16)
        value = lax.dot_general(
            jnp.concatenate([own, beyond], axis=1), sp[...], (((0,), (0,)), ((), ())), preferred_element_type=F32
        )
        value = value[:, 0:128] + value[:, 128:256]
        high = value.astype(BF16)
        low = (value - high.astype(F32)).astype(BF16)
        value = jnp.dot(pz[...], jnp.concatenate([high[0:128], low[0:128]], axis=0), preferred_element_type=F32)
        value = (value * (1.0 / 3.0)).reshape(8, 32, 128)
        outside = jnp.dot(ph[...], jnp.concatenate([high[128:256], low[128:256]], axis=0), preferred_element_type=F32)
        outside = outside * (1.0 / 3.0)
        edge = jnp.dot(ey[...], own, preferred_element_type=F32)
        high = edge.astype(BF16)
        low = (edge - high.astype(F32)).astype(BF16)
        edge = jnp.concatenate([high, low], axis=0)
        edge = [jnp.dot(edge, kxz[128 * i : 128 * i + 128, :], preferred_element_type=F32) for i in range(2)]
        edge = [(part[0:8] + part[16:24]) * (1.0 / 9.0) for part in edge]
        for e in range(4):
            one, two = value[2 * e], value[2 * e + 1]
            mixed = (one, one * (2.0 / 3.0) + two * (1.0 / 3.0), one * (1.0 / 3.0) + two * (2.0 / 3.0), two)
            for j in range(4):
                after[4 * e + j] = after[4 * e + j] + mixed[j]
            part = edge[e // 2][:, 128 * (e % 2) : 128 * (e % 2) + 128]
            yadd[5, e : e + 1, :] = part[0:1]
            yadd[5, 4 + e : 5 + e, :] = part[1:2]
        fused(
            after,
            resid_ref if final else r,
            [x_sides[0] + outside[0:32], x_sides[1] + outside[32:64]],
            [z_sides[0] + outside[64:80], z_sides[1] + outside[80:96]],
            y_rows + yadd[5],
            final,
        )
        back_all.wait_send()


def body(forcing, start, element_class_index, class_coef):
    consts = [jnp.asarray(t) for t in tables()]
    eigen_y = consts.pop()
    full, brick = (16, 32, 128), (4, 32, 128)
    vmem = pltpu.VMEM
    dma = pltpu.SemaphoreType.DMA
    scratch = (
        [vmem(full, F32), vmem((2,) + full, F32), vmem((2,) + full, F32), vmem(full, F32), vmem(full, F32)]
        + [vmem(brick, F32)] * 3
        + [vmem(full, F32)] * 2
        + [vmem((17, 32, 128), F32), vmem((2, 32, 128), F32)]
        + [vmem(brick, F32)] * 2
        + [vmem((2, 4, 8, 128), F32)]
        + [vmem(brick, F32)] * 3
        + [vmem((32, 32), jnp.int32), pltpu.SMEM((3, 16), F32), pltpu.SMEM((256,), F32)]
        + [vmem((5, 112, 128), F32), vmem((5, 2, 16, 128), F32), vmem((5, 8, 128), F32)]
        + [vmem((96, 128), F32), vmem((8, 128), F32), vmem((8, 128), F32), vmem((6, 8, 128), F32)]
        + [vmem((1120, 256), BF16), vmem((528, 256), BF16), vmem((32, 256), BF16)]
        + [vmem((128, 128), F32), vmem((256, 512), F32)]
        + [vmem((256, 256), BF16), vmem((64, 128), F32), vmem((128, 128), F32)]
        + [vmem((2, 32, 8, 128), BF16), vmem((2, 32, 8, 128), BF16), vmem((2, 16, 4, 16, 128), BF16)]
        + [vmem((2, 32, 2, 8, 128), BF16), vmem((2, 8, 2, 8, 128), BF16)]
        + [dma((9,)), dma((5,)), dma((5,)), dma((1,)), dma((1,))]
        + [dma((2,))] * 6
    )
    anywhere = pl.BlockSpec(memory_space=pl.ANY)
    shape = pltpu.VMEM(full, F32)
    return pl.pallas_call(
        kernel,
        out_shape=(shape, shape),
        in_specs=[anywhere] * 9,
        out_specs=(pl.BlockSpec(memory_space=pltpu.VMEM),) * 2,
        scratch_shapes=scratch,
        compiler_params=pltpu.CompilerParams(collective_id=0, has_side_effects=True),
        name="cycles",
    )(forcing, start, element_class_index.reshape(32, 32), class_coef, eigen_y, *consts)


def solution(mesh):
    spec = P("bx", "bz", "by")
    return jax.shard_map(
        body, mesh=mesh, in_specs=(spec, spec, spec, P()), out_specs=(spec, spec), check_vma=False
    )
```

```python
import math

import jax
import jax.numpy as jnp
import numpy as np
from jax import lax
from jax.experimental import pallas as pl
from jax.experimental.pallas import tpu as pltpu
from jax.sharding import PartitionSpec as P

CYCLES = 2
DAMPING = 0.6666666666666666
NBX, NBY, NBZ = 16, 4, 8
CX, CZ, CY = 128, 128, 256
F32, BF16 = jnp.float32, jnp.bfloat16
MESH = pl.DeviceIdType.MESH
OFFSETS = sorted(
    ((a, b) for a in range(4) for b in range(4) if (a, b) != (0, 0)),
    key=lambda o: -(min(o[0], 4 - o[0]) + 2 * min(o[1], 4 - o[1])),
)


PLANE = [(a, b) for b in (4, 3, 5, 2, 6, 1, 7, 0) for a in (2, 3, 1, 0) if (a, b) != (0, 0)]


ROWS = {
    "rz": slice(0, 128), "pz": slice(128, 384), "fx": slice(384, 640),
    "ph": slice(640, 736), "kxz": slice(736, 992), "sz": slice(992, 1120),
}


def rounded(value):
    return np.asarray(value, dtype=np.float64).astype(np.float32).astype(jnp.bfloat16)


def sine(count):
    index = np.arange(1, count + 1, dtype=np.float64)
    table = np.sin(np.outer(index, index) * (math.pi / (count + 1))) * math.sqrt(2.0 / (count + 1))
    return rounded(table).astype(np.float64)


def spectrum(count):
    return 2.0 - 2.0 * np.cos(np.arange(1, count + 1) * (math.pi / (count + 1)))


def split(value):
    high = rounded(value)
    return high, rounded(value - high.astype(np.float64))


def tables():
    sine_x, sine_z, sine_y = sine(CX), sine(CZ), sine(CY)
    steps = np.array([[3.0, 2.0, 1.0, 0.0], [0.0, 1.0, 2.0, 3.0]])
    restrict_z = np.kron(np.eye(64), steps)
    prolong_z = np.concatenate([restrict_z.T, restrict_z.T], axis=1)
    blocks = sine_x.reshape(CX, NBX, 8)
    forward_x = np.zeros((2, CX, NBX, 2, 8))
    inverse_x = np.zeros((NBX, 2, 16, 2, CX))
    for member in range(2):
        forward_x[member, :, :, member, :] = blocks
        inverse_x[:, member, :8, member, :] = sine_x.reshape(NBX, 8, CX)
        inverse_x[1:, member, 8, member, :] = sine_x[7:-1:8]
        inverse_x[:-1, member, 9, member, :] = sine_x[8::8]
    along_y = np.kron(np.eye(CY // 2), steps)
    spread = (sine_y @ along_y / 3.0).reshape(CY, NBY, 128).transpose(1, 0, 2)
    spread = np.concatenate(split(spread), axis=2)
    gather = (sine_y.reshape(CY, NBY, 64).transpose(1, 0, 2) @ np.kron(np.eye(32), steps)) / 6.0
    gather = np.concatenate(split(gather), axis=2)
    edge_y = np.zeros((NBY, 16, CY))
    edge_y[1:, 0] = sine_y[63:-1:64]
    edge_y[:-1, 1] = sine_y[64::64]
    halo = np.zeros((96, 128))
    for side in range(2):
        halo[32 * side : 32 * side + 32, 16 * side : 16 * side + 16] = np.kron(np.eye(8), steps).T
        halo[64 + 16 * side : 80 + 16 * side, 32 + 16 * side : 40 + 16 * side] = np.kron(np.eye(4), steps).T
    halo = np.concatenate([halo, halo], axis=1)
    plane_xz = np.kron(np.kron(np.eye(4), steps), np.kron(np.eye(8), steps))
    plane = (spectrum(CX)[:, None] + spectrum(CZ)[None, :]).astype(np.float32)
    common = np.zeros((1120, 256))
    for name, value in (("rz", restrict_z), ("pz", prolong_z), ("fx", forward_x.reshape(256, 256)), ("ph", halo), ("sz", sine_z)):
        common[ROWS[name], : value.shape[1]] = value
    common[ROWS["kxz"]] = plane_xz.reshape(128, 2, 256).transpose(1, 0, 2).reshape(256, 256)
    along = np.concatenate([np.asarray(v, np.float64) for v in (gather, spread, edge_y)], axis=1)
    return (
        rounded(common),
        rounded(along),
        rounded(inverse_x.reshape(NBX, 32, 256)),
        plane,
        spectrum(CY).astype(np.float32),
    )


def turn(values, block):
    values = list(values)
    for bit in (4, 2, 1):
        low = (block & bit) == 0
        for first in range(8):
            if first & bit:
                continue
            second = first | bit
            one, two = values[first], values[second]
            values[first] = jnp.where(low, one, pltpu.roll(two, 16 * bit, 1))
            values[second] = jnp.where(low, pltpu.roll(one, 128 - 16 * bit, 1), two)
    return values


def kernel(
    forcing_hbm, start_hbm, class_hbm, coef_hbm, eigen_hbm, common_hbm, along_hbm, ix_hbm, plane_hbm,
    out_ref, resid_ref,
    f, s, z, r, inner, kap, beta, base, diag, dinv, wx, wxb, wzl, wzh, wzb, wyl, wyh, wyb,
    class_ref, coef, eigen_y, halos, zsend, ysend, khalo, kzsend, kysend, yadd,
    common, along, ix, plane, invlam, fine, swap, wide_swap,
    va, vsend, xg, vb, vbsend,
    load_sem, halo_s, halo_r, kap_s, kap_r, z1_s, z1_r, x_s, x_r, z2_s, z2_r,
):
    ib, iy, iz = lax.axis_index("bx"), lax.axis_index("by"), lax.axis_index("bz")
    loads = [
        pltpu.make_async_copy(src, dst, load_sem.at[i])
        for i, (src, dst) in enumerate(
            [
                (start_hbm, s.at[0]), (class_hbm, class_ref), (coef_hbm, coef), (eigen_hbm, eigen_y),
                (plane_hbm, plane), (forcing_hbm, f),
                (common_hbm, common), (along_hbm.at[iy], along), (ix_hbm.at[ib], ix),
            ]
        )
    ]
    def x_peer(offset):
        return lax.rem(ib // 4 + offset[0], 4) * 4 + lax.rem(lax.rem(ib, 4) + offset[1], 4)

    def plane_peer(offset):
        return lax.rem(iy + offset[0], NBY), lax.rem(iz + offset[1], NBZ)

    barrier = pltpu.get_barrier_semaphore()

    def greet(x_offsets, plane_offsets):
        for offset in x_offsets:
            pl.semaphore_signal(barrier, inc=1, device_id={"bx": x_peer(offset)}, device_id_type=MESH)
        for offset in plane_offsets:
            py, pz_ = plane_peer(offset)
            pl.semaphore_signal(barrier, inc=1, device_id={"by": py, "bz": pz_}, device_id_type=MESH)

    near_x, near_plane = [(0, 1), (0, 3), (1, 1), (3, 3)], [(0, 1), (0, 7), (1, 0), (3, 0)]
    greet(near_x, near_plane)
    loads[0].start()
    loads[1].start()
    loads[2].start()
    greet([o for o in OFFSETS if o not in near_x], [o for o in PLANE if o not in near_plane])
    for load in loads[3:]:
        load.start()

    row = lax.broadcasted_iota(jnp.int32, (32, 128), 0)
    lane = lax.broadcasted_iota(jnp.int32, (32, 128), 1)
    spread_y = (lax.broadcasted_iota(jnp.int32, (32, 128), 1) // 4 == row).astype(F32).astype(BF16)
    tall = lax.broadcasted_iota(jnp.int32, (128, 32), 0) // 4
    spread_z = (tall == lax.broadcasted_iota(jnp.int32, (128, 32), 1)).astype(F32).astype(BF16)
    loads[1].wait()
    loads[2].wait()
    labels = class_ref[...].astype(F32).astype(BF16)
    labels = jnp.dot(labels, spread_y, preferred_element_type=F32).astype(BF16)
    labels = jnp.dot(spread_z, labels, preferred_element_type=F32)
    kappa = jnp.zeros((128, 128), F32)
    sigma = jnp.zeros((128, 128), F32)
    cubic = jnp.zeros((128, 128), F32)
    for index in range(16):
        hit = labels == float(index)
        kappa = jnp.where(hit, coef[0, index], kappa)
        sigma = jnp.where(hit, coef[1, index], sigma)
        cubic = jnp.where(hit, coef[2, index], cubic)
    kap[...] = kappa.reshape(4, 32, 128)
    base[...] = sigma.reshape(4, 32, 128)
    beta[...] = cubic.reshape(4, 32, 128)
    kysend[...] = jnp.transpose(pltpu.roll(kappa, 1, 1))[0:8]
    kzsend[0:4] = kap[:, 0, :]
    kzsend[4:8] = kap[:, 31, :]

    def pack(field, slot):
        wide = lax.broadcasted_iota(jnp.int32, (128, 128), 1)
        edge = jnp.zeros((128, 128), F32)
        for e in range(4):
            part = field[4 * e : 4 * e + 4].reshape(128, 128)
            edge = jnp.where(wide // 2 == e, pltpu.roll(part, 1 + 2 * e, 1), edge)
        ysend[slot] = jnp.transpose(edge)[0:8]
        zsend[slot, 0] = field[:, 0, :]
        zsend[slot, 1] = field[:, 31, :]

    xa, xb = lax.rem(ib + 15, NBX), lax.rem(ib + 1, NBX)
    ya, yb = lax.rem(iy + 3, NBY), lax.rem(iy + 1, NBY)
    za, zb = lax.rem(iz + 7, NBZ), lax.rem(iz + 1, NBZ)

    def remote(src, dst, send, recv, device):
        return pltpu.make_async_remote_copy(
            src_ref=src, dst_ref=dst, send_sem=send, recv_sem=recv, device_id=device, device_id_type=MESH
        )

    def halo(field, slot):
        to, ss, rs = halos.at[slot], halo_s.at[slot], halo_r.at[slot]
        return [
            remote(field.at[0], to.at[32:64], ss, rs, {"bx": xa}),
            remote(field.at[15], to.at[0:32], ss, rs, {"bx": xb}),
            remote(zsend.at[slot, 0], to.at[80:96], ss, rs, {"bz": za}),
            remote(zsend.at[slot, 1], to.at[64:80], ss, rs, {"bz": zb}),
            remote(ysend.at[slot], to.at[104:112], ss, rs, {"by": ya}),
            remote(ysend.at[slot], to.at[96:104], ss, rs, {"by": yb}),
        ]

    def halo_wait(slot):
        remote(halos.at[slot], halos.at[slot], halo_s.at[slot], halo_r.at[slot], {"bx": xa}).wait()

    loads[0].wait()
    pack(s.at[0], 0)
    kappa_copies = [
        remote(kap.at[0], khalo.at[32:64], kap_s.at[0], kap_r.at[0], {"bx": xa}),
        remote(kap.at[3], khalo.at[0:32], kap_s.at[0], kap_r.at[0], {"bx": xb}),
        remote(kzsend, khalo.at[72:80], kap_s.at[0], kap_r.at[0], {"bz": za}),
        remote(kzsend, khalo.at[64:72], kap_s.at[0], kap_r.at[0], {"bz": zb}),
        remote(kysend, khalo.at[88:96], kap_s.at[0], kap_r.at[0], {"by": ya}),
        remote(kysend, khalo.at[80:88], kap_s.at[0], kap_r.at[0], {"by": yb}),
    ]
    pl.semaphore_wait(barrier, len(OFFSETS) + len(PLANE))
    for copy in kappa_copies:
        copy.start()
    for copy in halo(s.at[0], 0):
        copy.start()

    zero = jnp.zeros((32, 128), F32)
    for e in range(4):
        k = kap[e]
        first, second, third = (row % 4 == 0), (row % 4 == 3), (lane % 4 == 0)
        zl = jnp.where(row == 0, zero, jnp.where(first, pltpu.roll(k, 1, 0) + k, k))
        zu = jnp.where(row == 31, zero, jnp.where(second, pltpu.roll(k, 31, 0) + k, k))
        yl = jnp.where(lane == 0, zero, jnp.where(third, pltpu.roll(k, 1, 1) + k, k))
        yu = jnp.where(lane == 127, zero, jnp.where(lane % 4 == 3, pltpu.roll(k, 127, 1) + k, k))
        wzl[e], wzh[e], wyl[e], wyh[e] = zl, zu, yl, yu
        base[e] = base[e] + ((zl + zu) + (yl + yu))
        for j in range(4):
            if j > 0:
                wx[4 * e + j] = k
            elif e > 0:
                wx[4 * e] = kap[e - 1] + k
    wx[0] = zero
    wx[16] = zero

    def inner_sum(field):
        def step(e, carry):
            zl, zu, yl, yu = wzl[e], wzh[e], wyl[e], wyh[e]
            for j in range(4):
                x = 4 * e + j
                v = field[x]
                total = zl * pltpu.roll(v, 1, 0) + zu * pltpu.roll(v, 31, 0)
                total = total + yl * pltpu.roll(v, 1, 1) + yu * pltpu.roll(v, 127, 1)
                total = total + wx[x] * field[lax.rem(x + 15, 16)]
                total = total + wx[x + 1] * field[lax.rem(x + 1, 16)]
                inner[x] = total
            return carry

        lax.fori_loop(0, 4, step, 0)

    inner_sum(s.at[0])

    kbar, sbar = coef[0, 0], coef[1, 0]
    for index in range(1, 16):
        kbar, sbar = kbar + coef[0, index], sbar + coef[1, index]
    kbar, sbar = kbar * 0.0625, sbar * 0.0625
    loads[3].wait()
    loads[4].wait()
    mode = iy * 64 + iz * 8
    for member in range(2):
        for pair in range(4):
            value = kbar * (plane[...] + eigen_y[mode + 2 * pair + member]) + sbar
            invlam[pl.ds(member * 128, 128), pl.ds(pair * 128, 128)] = 1.0 / value

    def inside(flag):
        return jnp.where(flag, 1.0, 0.0).astype(F32)

    x_in = (inside(ib > 0), inside(ib < NBX - 1))
    z_in = (inside(iz > 0), inside(iz < NBZ - 1))
    y_in = (inside(iy > 0), inside(iy < NBY - 1))
    remote(khalo, khalo, kap_s.at[0], kap_r.at[0], {"bx": xa}).wait()
    row8 = lax.broadcasted_iota(jnp.int32, (8, 128), 0)
    ends = []
    for side, e in ((0, 0), (1, 3)):
        weight = kap[e] + khalo[32 * side : 32 * side + 32] * x_in[side]
        wxb[side] = weight * x_in[side]
        ends.append(weight)
    low_y = jnp.transpose(khalo[80:88])[:, 0:1]
    high_y = jnp.transpose(khalo[88:96])[:, 1:2]
    wide = lax.broadcasted_iota(jnp.int32, (128, 128), 1)
    outer = jnp.where(wide == 0, y_in[0], jnp.where(wide == 127, y_in[1], 0.0))
    other = jnp.where(wide == 0, jnp.broadcast_to(low_y, (128, 128)), jnp.broadcast_to(high_y, (128, 128)))
    edge_y = (wide == 0) | (wide == 127)
    edge_y = jnp.where(edge_y, kap[...].reshape(128, 128) + other * outer, 0.0)
    wyb[...] = (edge_y * outer).reshape(4, 32, 128)
    base[...] = base[...] + edge_y.reshape(4, 32, 128)
    for e in range(4):
        low = jnp.where(row8 == 0, kap[e, 0:8, :] + khalo[68 + e : 69 + e, :] * z_in[0], 0.0)
        high = jnp.where(row8 == 7, kap[e, 24:32, :] + khalo[72 + e : 73 + e, :] * z_in[1], 0.0)
        wzb[0, e] = low * z_in[0]
        wzb[1, e] = high * z_in[1]
        base[e, 0:8, :] = base[e, 0:8, :] + low
        base[e, 24:32, :] = base[e, 24:32, :] + high
    for x in range(16):
        below = ends[0] if x == 0 else wx[x]
        above = ends[1] if x == 15 else wx[x + 1]
        total = base[x // 4] + (below + above)
        diag[x] = total

    def outer_sum(x_sides, z_sides, y_rows):
        inner[0] = inner[0] + wxb[0] * x_sides[0]
        inner[15] = inner[15] + wxb[1] * x_sides[1]
        columns = jnp.transpose(y_rows)
        wide = lax.broadcasted_iota(jnp.int32, (128, 128), 1)
        for e in range(4):
            low = jnp.broadcast_to(columns[:, e : e + 1], (128, 128))
            high = jnp.broadcast_to(columns[:, 4 + e : 5 + e], (128, 128))
            other = jnp.where(wide == 0, low, high).reshape(4, 32, 128)
            weight = wyb[e]
            for j in range(4):
                x = 4 * e + j
                inner[x] = inner[x] + weight * other[j]
                inner[x, 0:8, :] = inner[x, 0:8, :] + wzb[0, e] * z_sides[0][x : x + 1, :]
                inner[x, 24:32, :] = inner[x, 24:32, :] + wzb[1, e] * z_sides[1][x : x + 1, :]

    def arrived(slot):
        for e in range(4):
            yadd[slot, e : e + 1, :] = halos[slot, 96 + 2 * e : 97 + 2 * e, :]
            yadd[slot, 4 + e : 5 + e, :] = halos[slot, 105 + 2 * e : 106 + 2 * e, :]
        got = halos[slot, 0:96, :]
        return [got[0:32], got[32:64]], [got[64:80], got[80:96]], yadd[slot]

    def restricted(e, planes):
        one, two, three, four = planes
        for half, value in ((0, 3.0 * one + 2.0 * two + three), (1, two + 2.0 * three + 3.0 * four)):
            high = value.astype(BF16)
            at = pl.ds((2 * e + half) * 32, 32)
            fine[at, 0:128] = high
            fine[at, 128:256] = (value - high.astype(F32)).astype(BF16)

    def fused(field, store, x_sides, z_sides, y_rows, last):
        columns = jnp.transpose(y_rows)
        wide = lax.broadcasted_iota(jnp.int32, (128, 128), 1)
        for e in range(4):
            low = jnp.broadcast_to(columns[:, e : e + 1], (128, 128))
            high = jnp.broadcast_to(columns[:, 4 + e : 5 + e], (128, 128))
            other = jnp.where(wide == 0, low, high).reshape(4, 32, 128)
            planes = []
            for j in range(4):
                x = 4 * e + j
                v = field[x]
                total = wzl[e] * pltpu.roll(v, 1, 0) + wzh[e] * pltpu.roll(v, 31, 0)
                total = total + wyl[e] * pltpu.roll(v, 1, 1) + wyh[e] * pltpu.roll(v, 127, 1)
                total = total + wyb[e] * other[j]
                total = total + (wxb[0] * x_sides[0] if x == 0 else wx[x] * field[x - 1])
                total = total + (wxb[1] * x_sides[1] if x == 15 else wx[x + 1] * field[x + 1])
                low_z = total[0:8] + wzb[0, e] * z_sides[0][x : x + 1, :]
                high_z = total[24:32] + wzb[1, e] * z_sides[1][x : x + 1, :]
                total = jnp.concatenate([low_z, total[8:24], high_z], axis=0)
                value = (f[x] - (diag[x] * v - total)) - beta[e] * v * v * v
                store[x] = value
                planes.append(value)
            if not last:
                restricted(e, planes)

    def residual(field, store):
        for e in range(4):
            cube = beta[e]
            planes = []
            for j in range(4):
                x = 4 * e + j
                v = field[x]
                value = (f[x] - (diag[x] * v - inner[x])) - cube * v * v * v
                store[x] = value
                planes.append(value)
            restricted(e, planes)

    block = lax.broadcasted_iota(jnp.int32, (8, 128), 1) // 16
    for load in loads[5:]:
        load.wait()
    halo_wait(0)
    outer_sum(*arrived(0))
    residual(s.at[0], r)
    rz, pz, fx, ph = (common.at[ROWS[name]] for name in ("rz", "pz", "fx", "ph"))
    sz = common.at[ROWS["sz"], 0:128]
    kxz = common.at[ROWS["kxz"]]
    gy, sp, ey = along.at[0:256], along.at[256:512], along.at[512:528]
    lane8 = lax.broadcasted_iota(jnp.int32, (8, 128), 1)
    me = iy * NBZ + iz

    for cycle in range(CYCLES):
        value = jnp.dot(rz[...], fine[...], preferred_element_type=F32)
        value = ((value[:, 0:128] + value[:, 128:256]) * (1.0 / 36.0)).astype(BF16)
        value = jnp.concatenate([value, value], axis=1)
        value = lax.dot_general(gy[...], value, (((1,), (1,)), ((), ())), preferred_element_type=F32)
        vsend[cycle] = value.reshape(32, 8, 128).astype(BF16)

        def forward(offset):
            py, pz_ = plane_peer(offset)
            return remote(
                vsend.at[cycle, py * NBZ + pz_], va.at[cycle, me], z1_s.at[cycle], z1_r.at[cycle], {"by": py, "bz": pz_}
            )

        for o in PLANE:
            forward(o).start()
        va[cycle, me] = vsend[cycle, me]

        smooth = z.at[cycle]
        if cycle == 0:
            dinv[...] = DAMPING / diag[...]
        smooth[...] = r[...] * dinv[...]
        pack(smooth, 2 * cycle + 1)
        for copy in halo(smooth, 2 * cycle + 1):
            copy.start()
        inner_sum(smooth)
        some = va.at[cycle, pl.ds(0, 31)]
        forward_all = remote(some, some, z1_s.at[cycle], z1_r.at[cycle], {"bz": zb})
        forward_all.wait_recv()
        parts = []
        for i in range(8):
            one, two, three, four = (va[cycle, 8 * j + i].astype(F32) for j in range(4))
            parts.append((one + two) + (three + four))
        value = jnp.concatenate(turn(parts, block), axis=0).astype(BF16)
        swap[...] = jnp.dot(value, sz[...], preferred_element_type=F32)
        value = jnp.concatenate([swap[pl.ds(m, 8, stride=8), :] for m in range(8)], axis=0)
        xg[cycle, ib] = value.reshape(4, 16, 128).astype(BF16)
        for o in OFFSETS:
            remote(xg.at[cycle, ib], xg.at[cycle, ib], x_s.at[cycle], x_r.at[cycle], {"bx": x_peer(o)}).start()
        forward_all.wait_send()

        final = cycle == CYCLES - 1
        after = out_ref if final else s.at[cycle + 1]
        halo_wait(2 * cycle + 1)
        outer_sum(*arrived(2 * cycle + 1))
        after[...] = s[cycle] + ((2.0 - DAMPING) * smooth[...] + dinv[...] * inner[...])
        pack(after, 2 * cycle + 2)
        some = xg.at[cycle, pl.ds(0, 15)]
        x_all = remote(some, some, x_s.at[cycle], x_r.at[cycle], {"bx": xa})
        x_all.wait_recv()
        parts = []
        for half in range(2):
            value = jnp.concatenate(
                [xg[cycle, :, 2 * half + i, :, :].reshape(256, 128) for i in range(2)], axis=1
            )
            value = jnp.dot(fx[...], value, preferred_element_type=F32)
            value = (value * invlam[:, 256 * half : 256 * half + 256]).astype(BF16)
            value = jnp.dot(ix[...], value, preferred_element_type=F32)
            parts += [value[:, 0:128], value[:, 128:256]]
        value = jnp.concatenate(parts, axis=0).astype(BF16)
        wide_swap[...] = jnp.dot(value, sz[...], preferred_element_type=F32)
        lines = [wide_swap[pl.ds(i, 8, stride=16), :] for i in range(10)]
        low = high = none = jnp.zeros((8, 128), F32)
        for i in range(8):
            low = jnp.where(lane8 % 16 == i, pltpu.roll(lines[i], 1 + i, 1), low)
            high = jnp.where(lane8 % 16 == i, pltpu.roll(lines[i], 112 + i, 1), high)
        own = turn(lines[0:8], block)
        beyond = turn([lines[8], lines[9], low, high, none, none, none, none], block)
        for i in range(8):
            vbsend[cycle, i, 0] = own[i].astype(BF16)
            vbsend[cycle, i, 1] = beyond[i].astype(BF16)

        def backward(offset):
            py, pz_ = plane_peer(offset)
            return remote(
                vbsend.at[cycle, pz_], vb.at[cycle, me], z2_s.at[cycle], z2_r.at[cycle], {"by": py, "bz": pz_}
            )

        for o in PLANE:
            backward(o).start()
        for copy in halo(after, 2 * cycle + 2):
            copy.start()
        vb[cycle, me] = vbsend[cycle, iz]
        x_all.wait_send()
        halo_wait(2 * cycle + 2)
        x_sides, z_sides, y_rows = arrived(2 * cycle + 2)
        some = vb.at[cycle, pl.ds(0, 31)]
        back_all = remote(some, some, z2_s.at[cycle], z2_r.at[cycle], {"bz": zb})
        back_all.wait_recv()

        own = vb[cycle, :, 0].astype(F32).reshape(CY, 128).astype(BF16)
        beyond = vb[cycle, :, 1].astype(F32).reshape(CY, 128).astype(BF16)
        value = lax.dot_general(
            jnp.concatenate([own, beyond], axis=1), sp[...], (((0,), (0,)), ((), ())), preferred_element_type=F32
        )
        value = value[:, 0:128] + value[:, 128:256]
        high = value.astype(BF16)
        low = (value - high.astype(F32)).astype(BF16)
        value = jnp.dot(pz[...], jnp.concatenate([high[0:128], low[0:128]], axis=0), preferred_element_type=F32)
        value = (value * (1.0 / 3.0)).reshape(8, 32, 128)
        outside = jnp.dot(ph[...], jnp.concatenate([high[128:256], low[128:256]], axis=0), preferred_element_type=F32)
        outside = outside * (1.0 / 3.0)
        edge = jnp.dot(ey[...], own, preferred_element_type=F32)
        high = edge.astype(BF16)
        low = (edge - high.astype(F32)).astype(BF16)
        edge = jnp.concatenate([high, low], axis=0)
        edge = [jnp.dot(edge, kxz[128 * i : 128 * i + 128, :], preferred_element_type=F32) for i in range(2)]
        edge = [(part[0:8] + part[16:24]) * (1.0 / 9.0) for part in edge]
        for e in range(4):
            one, two = value[2 * e], value[2 * e + 1]
            mixed = (one, one * (2.0 / 3.0) + two * (1.0 / 3.0), one * (1.0 / 3.0) + two * (2.0 / 3.0), two)
            for j in range(4):
                after[4 * e + j] = after[4 * e + j] + mixed[j]
            part = edge[e // 2][:, 128 * (e % 2) : 128 * (e % 2) + 128]
            yadd[5, e : e + 1, :] = part[0:1]
            yadd[5, 4 + e : 5 + e, :] = part[1:2]
        fused(
            after,
            resid_ref if final else r,
            [x_sides[0] + outside[0:32], x_sides[1] + outside[32:64]],
            [z_sides[0] + outside[64:80], z_sides[1] + outside[80:96]],
            y_rows + yadd[5],
            final,
        )
        back_all.wait_send()


def body(forcing, start, element_class_index, class_coef):
    consts = [jnp.asarray(t) for t in tables()]
    eigen_y = consts.pop()
    full, brick = (16, 32, 128), (4, 32, 128)
    vmem = pltpu.VMEM
    dma = pltpu.SemaphoreType.DMA
    scratch = (
        [vmem(full, F32), vmem((2,) + full, F32), vmem((2,) + full, F32), vmem(full, F32), vmem(full, F32)]
        + [vmem(brick, F32)] * 3
        + [vmem(full, F32)] * 2
        + [vmem((17, 32, 128), F32), vmem((2, 32, 128), F32)]
        + [vmem(brick, F32)] * 2
        + [vmem((2, 4, 8, 128), F32)]
        + [vmem(brick, F32)] * 3
        + [vmem((32, 32), jnp.int32), pltpu.SMEM((3, 16), F32), pltpu.SMEM((256,), F32)]
        + [vmem((5, 112, 128), F32), vmem((5, 2, 16, 128), F32), vmem((5, 8, 128), F32)]
        + [vmem((96, 128), F32), vmem((8, 128), F32), vmem((8, 128), F32), vmem((6, 8, 128), F32)]
        + [vmem((1120, 256), BF16), vmem((528, 256), BF16), vmem((32, 256), BF16)]
        + [vmem((128, 128), F32), vmem((256, 512), F32)]
        + [vmem((256, 256), BF16), vmem((64, 128), F32), vmem((128, 128), F32)]
        + [vmem((2, 32, 8, 128), BF16), vmem((2, 32, 8, 128), BF16), vmem((2, 16, 4, 16, 128), BF16)]
        + [vmem((2, 32, 2, 8, 128), BF16), vmem((2, 8, 2, 8, 128), BF16)]
        + [dma((9,)), dma((5,)), dma((5,)), dma((1,)), dma((1,))]
        + [dma((2,))] * 6
    )
    anywhere = pl.BlockSpec(memory_space=pl.ANY)
    shape = pltpu.VMEM(full, F32)
    return pl.pallas_call(
        kernel,
        out_shape=(shape, shape),
        in_specs=[anywhere] * 9,
        out_specs=(pl.BlockSpec(memory_space=pltpu.VMEM),) * 2,
        scratch_shapes=scratch,
        compiler_params=pltpu.CompilerParams(collective_id=0, has_side_effects=True),
        name="cycles",
    )(forcing, start, element_class_index.reshape(32, 32), class_coef, eigen_y, *consts)


def solution(mesh):
    spec = P("bx", "bz", "by")
    return jax.shard_map(
        body, mesh=mesh, in_specs=(spec, spec, spec, P()), out_specs=(spec, spec), check_vma=False
    )
```
